32 devices in a mesh: groups: 2 (over y), tm: 8 (over z, x), space: 2 (over core).
Axes of the slice: x: 2, y: 2, z: 4, core: 2. Of those that a mesh axis runs over, the one named last changes fastest.
Arguments:
- interior_diag: bfloat16 [24576, 1536], P(('groups', 'tm'), 'space'), parts along dimension 0, may hold values from -1 to 5, as said below
- coupling: bfloat16 [24576, 1536], P(('groups', 'tm'), 'space'), parts along dimension 0, may hold values from -0.29882812 to 0.29882812
- arrow_rows: bfloat16 [12288, 1536], P(('groups', 'tm', 'space')), parts along dimension 0, may hold values from -0.59765625 to 0.59765625
- separator_diag: bfloat16 [24576, 1536], P(('groups', 'tm'), 'space'), parts along dimension 0, may hold values from -1 to 5, as said below
- tip: bfloat16 [1536, 768], P('groups', 'space'), parts along dimension 0, may hold values from -6 to 6
- lengths: int32 [16], P('groups'), parts along dimension 0, may hold values from 1 to 2, 12 in all
Outputs:
- new_separator: bfloat16 [24576, 1536], P(('groups', 'tm'), 'space'), parts along dimension 0
- arrow_fill: bfloat16 [12288, 1536], P(('groups', 'tm'), 'space'), parts along dimension 0
- new_tip: float32 [1536, 768], P('groups', 'space'), parts along dimension 0
The draws below stay inside these ranges and needn't reach their ends.
There are 2 independent parts, one for each index of `groups`. The reference program is written for one: setup_inputs(seed, part) draws one part's arguments, and reference() takes and returns one part's arrays. A program takes and returns all parts, laid end to end along the dimension named above; each array names one. Nothing has to cross between parts.
Inputs may be any that keep to these rules, and one draw needn't show every extreme that they name: `interior_diag`: each block of 1536 rows is symmetric with eigenvalues above 0.5. `separator_diag`: each block of 1536 rows is symmetric with eigenvalues above 0.5. `lengths`: partition p has an interior block exactly when entry p is 2; some entry is 2.
All inputs are finite; a program needn't handle non-finite values.
Results may differ from the reference program's by a relative error of at most 0.008.
Values may be sent and summed in bfloat16 or wider, within the bound.
No kernel may reach another device: no remote copies, remote signals or barrier semaphores. Data moves between devices by JAX's collectives and lax.ppermute only.
A program may use at most 128 MiB of HBM per device.

```python
import math
import jax
import jax.numpy as jnp
import numpy as np
from jax import lax

B = 1536
A = 768
PARTITIONS = 8


def spd_blocks(key):
    noise_key, center_key = jax.random.split(key)
    noise_draw = jax.random.normal(noise_key, (PARTITIONS, B, B), jnp.float32)
    symmetric = (noise_draw + jnp.swapaxes(noise_draw, 1, 2)) * (0.5 / math.sqrt(B))
    center = jax.random.uniform(center_key, (PARTITIONS, B), jnp.float32, 2.0, 4.0)
    identity = jnp.eye(B, dtype=jnp.float32)
    return (symmetric + center[:, :, None] * identity[None, :, :]).reshape(PARTITIONS * B, B)


def draw_interior_diag(key, part):
    return spd_blocks(jax.random.fold_in(key, 11)).astype(jnp.bfloat16)


def draw_separator_diag(key, part):
    return spd_blocks(jax.random.fold_in(key, 23)).astype(jnp.bfloat16)


def steps_of(own_key, extent, cuts, low, high):
    def one(dim, parts):
        heights = jax.random.uniform(jax.random.fold_in(jax.random.fold_in(own_key, 6), dim), (parts,), jnp.float32, low / len(cuts), high / len(cuts))
        return jnp.repeat(jnp.exp(heights), extent[dim] // parts).reshape((-1,) + (1,) * (len(extent) - dim - 1))

    level = one(*cuts[0])
    for cut in cuts[1:]:
        level = level * one(*cut)
    return level


def profile(count, total, most, lean):
    weights = [(1 << 20) // math.isqrt(rank ** lean) + 1 for rank in range(2, count + 1)]
    rest, given = total - most - (count - 1), [1] * (count - 1)
    while rest > 0:
        candidates = [i for i in range(count - 1) if given[i] < most]
        mass, remaining = sum([weights[i] for i in candidates]), rest
        for i in candidates:
            extra = min(most - given[i], max(1, remaining * weights[i] // mass), rest)
            given[i] = given[i] + extra
            rest = rest - extra
    return np.array([most] + given)


def ragged(rng, number_of, total, most, skew):
    if number_of == 2:
        one = jax.random.randint(rng, (), max(1, total - most), min(most, total - 1) + 1)
        return jnp.stack([one, total - one])
    sizes = jnp.asarray(profile(number_of, total, most, skew), jnp.int32)
    pairs = (number_of - 1) // 2
    source_of, receiver = sizes[1:1 + 2 * pairs:2], sizes[2:2 + 2 * pairs:2]
    room = jnp.minimum(source_of - 1, most - receiver)
    moved = jax.random.randint(jax.random.fold_in(rng, 1), (pairs,), 0, 1 << 20) % (room + 1)
    sizes = sizes.at[1:1 + 2 * pairs:2].set(source_of - moved).at[2:2 + 2 * pairs:2].set(receiver + moved)
    return sizes[jax.random.permutation(jax.random.fold_in(rng, 2), number_of)]


def noise(key, dims, deviation, limit, shards=(), held_as=jnp.bfloat16):
    level = steps_of(key, dims, shards, -0.22, 0.18) if shards else 1.0
    drawn = jax.random.normal(key, dims, jnp.float32) * deviation * level
    return jnp.minimum(jnp.maximum(drawn, -limit), limit).astype(held_as)


def setup_inputs(seed: int = 0, part: int = 0) -> dict:
    arg_keys = jax.random.split(jax.random.key(seed), 7)
    part_splits = jax.random.split(jax.random.fold_in(arg_keys[6], part), 7)
    interior_diag = draw_interior_diag(jax.random.fold_in(jax.random.fold_in(arg_keys[6], part), 71), part)
    coupling = noise(part_splits[1], (PARTITIONS * B, B), 0.05, 0.29882812, ((0, 8), (1, 2)))
    arrow_rows = noise(part_splits[2], (PARTITIONS * A, B), 0.1, 0.59765625, ((0, 16),))
    separator_diag = draw_separator_diag(jax.random.fold_in(jax.random.fold_in(arg_keys[6], part), 71), part)
    tip = noise(part_splits[4], (A, A), 1.0, 6.0, ((1, 2),))
    lengths = ragged(part_splits[5], PARTITIONS, PARTITIONS + PARTITIONS // 2, 2, 0).astype(jnp.int32)
    return dict(interior_diag=interior_diag, coupling=coupling, arrow_rows=arrow_rows, separator_diag=separator_diag, tip=tip, lengths=lengths)


def eliminate(operands):
    diag_block, couple, arrows, position, length = operands
    factor = jnp.linalg.cholesky(diag_block.astype(jnp.float32))
    couple = jnp.where(position == 0, jnp.zeros(couple.shape, jnp.float32), couple.astype(jnp.float32))
    right_sides = jnp.concatenate([couple, arrows.astype(jnp.float32).T], axis=1)
    solved = lax.linalg.triangular_solve(factor, right_sides, left_side=True, lower=True).astype(jnp.bfloat16)
    solved = jnp.where(length == 2, solved, jnp.zeros(solved.shape, jnp.bfloat16))
    solved_e = solved[:, :B]
    solved_r = solved[:, B:]
    boundary = jnp.dot(solved_e.T.astype(jnp.float32), solved_e.astype(jnp.float32), preferred_element_type=jnp.float32)
    arrow_term = (-jnp.dot(solved_r.T.astype(jnp.float32), solved_e.astype(jnp.float32), preferred_element_type=jnp.float32)).astype(jnp.bfloat16)
    tip_term = jnp.dot(solved_r.T.astype(jnp.float32), solved_r.astype(jnp.float32), preferred_element_type=jnp.float32)
    return (boundary, arrow_term, tip_term)

def reference(interior_diag, coupling, arrow_rows, separator_diag, tip, lengths):
    positions = jnp.arange(PARTITIONS, dtype=jnp.int32)
    boundary, arrow_term, tip_terms = lax.map(eliminate, (interior_diag.reshape(PARTITIONS, B, B), coupling.reshape(PARTITIONS, B, B), arrow_rows.reshape(PARTITIONS, A, B), positions, lengths.astype(jnp.int32)))
    later_boundary = jnp.concatenate([boundary[1:], jnp.zeros((1, B, B), jnp.float32)], axis=0)
    later_arrow = jnp.concatenate([arrow_term[1:], jnp.zeros((1, A, B), jnp.bfloat16)], axis=0)
    new_separator = (separator_diag.reshape(PARTITIONS, B, B).astype(jnp.float32) - later_boundary).astype(jnp.bfloat16).reshape(PARTITIONS * B, B)
    arrow_fill = later_arrow.reshape(PARTITIONS * A, B)
    new_tip = tip.astype(jnp.float32) - jnp.sum(tip_terms, axis=0)
    return (new_separator, arrow_fill, new_tip)
```

```python
import functools

import jax
import jax.numpy as jnp
from jax import lax
from jax.experimental import pallas as pl
from jax.experimental.pallas import tpu as pltpu
from jax.sharding import PartitionSpec as P

F32 = jnp.float32
BF16 = jnp.bfloat16
BLOCK = 256
NEAR = 0.03
MOST_STEPS = 60


def shifted(block, axis, distance):
    devices = range(lax.axis_size(axis))
    route = [(i - distance, i) for i in devices if i - distance in devices]
    return lax.ppermute(block, axis, route)


def split(x):
    high = x.astype(BF16)
    return high, (x - high.astype(F32)).astype(BF16)


def nn(a, b):
    return lax.dot_general(a, b, (((1,), (0,)), ((), ())), preferred_element_type=F32)


def nt(a, b):
    return lax.dot_general(a, b, (((1,), (1,)), ((), ())), preferred_element_type=F32)


def three(dot, a, b):
    return dot(a[0], b[0]) + (dot(a[0], b[1]) + dot(a[1], b[0]))


def inverse_root(a, unit_ref, root_ref):
    size = a.shape[0]
    rows = lax.broadcasted_iota(jnp.int32, (size, size), 0)
    columns = lax.broadcasted_iota(jnp.int32, (size, size), 1)
    on_diagonal = rows == columns
    identity = jnp.where(on_diagonal, 1.0, 0.0).astype(F32)
    diagonal = jnp.where(on_diagonal, a, 0.0)
    scale_row = lax.rsqrt(jnp.sum(diagonal, axis=0, keepdims=True))
    scale_column = lax.rsqrt(jnp.sum(diagonal, axis=1, keepdims=True))
    unit = a * scale_row * scale_column
    off = unit - identity
    off_square = nn(off.astype(BF16), off.astype(BF16))
    bound = jnp.sqrt(jnp.sqrt(jnp.sum(off_square * off_square)))
    c = jnp.minimum(1.0, 1.9 / (1.0 + bound))
    gap = c * off - (1.0 - c) * identity
    gap_square = c * c * off_square - (2 * c * (1 - c)) * off + ((1 - c) * (1 - c)) * identity
    first = (jnp.sqrt(c) * (identity - 0.5 * gap + 0.375 * gap_square)).astype(BF16)
    high, low = split(unit)
    product = split(nt(high, first) + nt(low, first))
    gap = nn(first, product[0]) + nn(first, product[1]) - identity
    gap_square = nn(gap.astype(BF16), gap.astype(BF16))
    change = split(0.375 * gap_square - 0.5 * gap)
    root_ref[...] = first.astype(F32) + (nn(change[0], first) + nn(change[1], first))
    unit_ref[...] = unit

    def far(state):
        return jnp.logical_and(state[0] > NEAR**4, state[1] < MOST_STEPS)

    def step(state):
        root = split(root_ref[...])
        product = split(three(nt, split(unit_ref[...]), root))
        gap = three(nn, root, product) - identity
        gap_square = nn(gap.astype(BF16), gap.astype(BF16))
        change = split(0.375 * gap_square - 0.5 * gap)
        root_ref[...] += three(nn, change, root)
        return jnp.sum(gap_square * gap_square), state[1] + 1

    lax.while_loop(far, step, (jnp.sum(gap_square * gap_square), jnp.int32(0)))
    return root_ref[...] * scale_row


def eliminate_kernel(
    flags, diag_ref, e_ref, r_ref, solved_e, solved_r,
    diag, left_e, left_r, high, low, high_t, low_t, unit_ref, root_ref,
):
    size = diag_ref.shape[0]
    block = unit_ref.shape[0]
    steps = size // block

    def at(i):
        return slice(i * block, (i + 1) * block)

    @pl.when(flags[0] == 0)
    def _():
        solved_e[...] = jnp.zeros_like(solved_e)
        solved_r[...] = jnp.zeros_like(solved_r)

    @pl.when(flags[0] != 0)
    def _():
        for i in range(steps):
            diag[at(i), i * block:] = diag_ref[at(i), i * block:].astype(F32)
        left_e[...] = jnp.where(flags[1] != 0, e_ref[...].astype(F32), 0.0)
        left_r[...] = r_ref[...].astype(F32)
        for k in range(steps):
            root = split(inverse_root(diag[at(k), at(k)], unit_ref, root_ref))
            part_e = split(three(nn, root, split(left_e[at(k), :])))
            solved_e[at(k), :] = part_e[0]
            part_r = split(three(nt, split(left_r[:, at(k)]), root))
            solved_r[:, at(k)] = part_r[0]
            for j in range(k + 1, steps):
                panel = three(nn, root, split(diag[at(k), at(j)]))
                high[:, at(j)], low[:, at(j)] = split(panel)
                high_t[at(j), :], low_t[at(j), :] = split(panel.T)
            for i in range(k + 1, steps):
                panel_t = (high_t[at(i), :], low_t[at(i), :])
                for j in range(i, steps):
                    diag[at(i), at(j)] -= three(nn, panel_t, (high[:, at(j)], low[:, at(j)]))
                left_e[at(i), :] -= three(nn, panel_t, part_e)
                left_r[:, at(i)] -= three(nn, part_r, (high[:, at(i)], low[:, at(i)]))


def eliminate(flags, diag, e, r):
    size, block = diag.shape[0], BLOCK
    vmem = pl.BlockSpec(memory_space=pltpu.VMEM)
    return pl.pallas_call(
        eliminate_kernel,
        out_shape=(
            jax.ShapeDtypeStruct(e.shape, BF16),
            jax.ShapeDtypeStruct(r.shape, BF16),
        ),
        in_specs=[pl.BlockSpec(memory_space=pltpu.SMEM), vmem, vmem, vmem],
        out_specs=(vmem, vmem),
        scratch_shapes=[
            pltpu.VMEM((size, size), F32),
            pltpu.VMEM(e.shape, F32),
            pltpu.VMEM(r.shape, F32),
            pltpu.VMEM((block, size), BF16),
            pltpu.VMEM((block, size), BF16),
            pltpu.VMEM((size, block), BF16),
            pltpu.VMEM((size, block), BF16),
            pltpu.VMEM((block, block), F32),
            pltpu.VMEM((block, block), F32),
        ],
        compiler_params=pltpu.CompilerParams(vmem_limit_bytes=58 * 2**20),
    )(flags, diag, e, r)


def gram_terms(local_e, local_r, full_e, full_r):
    boundary = jnp.einsum("kb,kc->bc", full_e, local_e, preferred_element_type=F32)
    arrow_term = -jnp.einsum("ak,kc->ac", full_r, local_e, preferred_element_type=F32)
    tip_term = jnp.einsum("ak,ck->ac", full_r, local_r, preferred_element_type=F32)
    return (boundary, arrow_term, tip_term)


def on_device(interior_diag, coupling, arrow_rows, separator_diag, tip, lengths):
    position = lax.axis_index("tm")
    flags = jnp.stack([lengths[position] == 2, position != 0]).astype(jnp.int32)
    whole_diag = lax.all_gather(interior_diag, "space", axis=1, tiled=True)
    solved_e, solved_r = eliminate(flags, whole_diag, coupling, arrow_rows)
    full_e = lax.all_gather(solved_e, "space", axis=1, tiled=True)
    full_r = lax.all_gather(solved_r, "space", axis=0, tiled=True)
    own_boundary, own_arrow, tip_term = gram_terms(solved_e, solved_r, full_e, full_r)
    boundary = shifted(own_boundary.astype(BF16), "tm", -1).astype(F32)
    arrow_fill = shifted(own_arrow.astype(BF16), "tm", -1)
    tip_sum = lax.psum(tip_term, "tm")
    new_separator = (separator_diag.astype(F32) - boundary).astype(BF16)
    new_tip = tip.astype(F32) - tip_sum
    return (new_separator, arrow_fill, new_tip)


def solution(mesh):
    return jax.shard_map(
        on_device,
        mesh=mesh,
        in_specs=(
            P(("groups", "tm"), "space"),
            P(("groups", "tm"), "space"),
            P(("groups", "tm", "space"), None),
            P(("groups", "tm"), "space"),
            P("groups", "space"),
            P("groups"),
        ),
        out_specs=(
            P(("groups", "tm"), "space"),
            P(("groups", "tm"), "space"),
            P("groups", "space"),
        ),
        check_vma=False,
    )
```

```python
import functools

import jax
import jax.numpy as jnp
from jax import lax
from jax.experimental import pallas as pl
from jax.experimental.pallas import tpu as pltpu
from jax.sharding import PartitionSpec as P

F32 = jnp.float32
BF16 = jnp.bfloat16
BLOCK = 256
NEAR = 0.03
MOST_STEPS = 60
STAGES = 7


def split(x):
    high = x.astype(BF16)
    return high, (x - high.astype(F32)).astype(BF16)


def nn(a, b):
    return lax.dot_general(a, b, (((1,), (0,)), ((), ())), preferred_element_type=F32)


def nt(a, b):
    return lax.dot_general(a, b, (((1,), (1,)), ((), ())), preferred_element_type=F32)


def three(dot, a, b):
    return dot(a[0], b[0]) + (dot(a[0], b[1]) + dot(a[1], b[0]))


def total(x):
    return jnp.sum(x, keepdims=True)


def places(size):
    rows = lax.broadcasted_iota(jnp.int32, (size, size), 0)
    columns = lax.broadcasted_iota(jnp.int32, (size, size), 1)
    return rows, columns


def diagonal_row(x, on_diagonal):
    return jnp.sum(jnp.where(on_diagonal, x, 0.0), axis=0, keepdims=True)


def unit_scaled(a, on_diagonal):
    diagonal = jnp.where(on_diagonal, a, 0.0)
    scale_row = lax.rsqrt(jnp.sum(diagonal, axis=0, keepdims=True))
    scale_column = lax.rsqrt(jnp.sum(diagonal, axis=1, keepdims=True))
    return a * scale_row * scale_column, scale_row


def first_root(off, off_square, identity):
    bound = jnp.sqrt(jnp.sqrt(total(off_square * off_square)))
    c = jnp.minimum(1.0, 1.9 / (1.0 + bound))
    gap = c * off - (1.0 - c) * identity
    gap_square = c * c * off_square - (2 * c * (1 - c)) * off + ((1 - c) * (1 - c)) * identity
    return (jnp.sqrt(c) * (identity - 0.5 * gap + 0.375 * gap_square)).astype(BF16)


def root_stages(a, on_diagonal, identity, result):
    unit, scale_row = unit_scaled(a, on_diagonal)
    off = unit - identity
    off_high = off.astype(BF16)
    high, low = split(unit)
    yield
    off_square = nn(off_high, off_high)
    yield
    first = first_root(off, off_square, identity)
    yield
    product = split(nt(high, first) + nt(low, first))
    yield
    gap = nn(first, product[0]) + nn(first, product[1]) - identity
    gap_high = gap.astype(BF16)
    yield
    gap_square = nn(gap_high, gap_high)
    change = split(0.375 * gap_square - 0.5 * gap)
    yield
    root = first.astype(F32) + (nn(change[0], first) + nn(change[1], first))
    result.append(split(root * scale_row))
    result.append(gap_square)


def root_until_near(a, on_diagonal, identity, unit_ref, root_ref):
    unit, scale_row = unit_scaled(a, on_diagonal)
    off = unit - identity
    off_square = nn(off.astype(BF16), off.astype(BF16))
    unit_ref[...] = unit
    root_ref[...] = first_root(off, off_square, identity).astype(F32)

    def far(state):
        return jnp.logical_and(jnp.logical_not(state[0] <= NEAR**4), state[1] < MOST_STEPS)

    def step(state):
        root = split(root_ref[...])
        product = split(three(nt, split(unit_ref[...]), root))
        gap = three(nn, root, product) - identity
        gap_square = nn(gap.astype(BF16), gap.astype(BF16))
        change = split(0.375 * gap_square - 0.5 * gap)
        root_ref[...] += three(nn, change, root)
        return jnp.sum(gap_square * gap_square), state[1] + 1

    lax.while_loop(far, step, (jnp.float32(1.0), jnp.int32(0)))
    return split(root_ref[...] * scale_row)


def interleave(stages, fillers):
    share = -(-len(fillers) // STAGES)
    for _ in stages:
        for filler in fillers[:share]:
            filler()
        fillers = fillers[share:]
    for filler in fillers:
        filler()


def factor_kernel(
    flags, own_d, other_d, r_hbm, out_high, out_low, solved_r,
    given, diag, r_in, left_r, high, low, factor_high, factor_low, near, unit_ref, root_ref, sems,
):
    size, block = diag.shape[0], unit_ref.shape[0]
    half = own_d.shape[1]
    steps = size // block
    core = flags[1]

    def at(i):
        return slice(i * block, (i + 1) * block)

    def arrival(i, which):
        source = own_d if which == 0 else other_d
        side = core if which == 0 else 1 - core
        columns = pl.ds(pl.multiple_of(side * half, half), half)
        return pltpu.make_async_copy(source.at[at(i), :], given.at[at(i), columns], sems.at[which, i])

    def departure(k, which):
        source, target = ((factor_high, out_high), (factor_low, out_low))[which]
        rows = slice(k * block, size)
        return pltpu.make_async_copy(source.at[rows, at(k)], target.at[rows, at(k)], sems.at[2 + which, k])

    rows, columns = places(block)
    on_diagonal = rows == columns
    identity = jnp.where(on_diagonal, 1.0, 0.0).astype(F32)
    r_copy = pltpu.make_async_copy(r_hbm, r_in, sems.at[4, 0])

    @pl.when(flags[0] == 0)
    def _():
        solved_r[...] = jnp.zeros_like(solved_r)

    @pl.when(flags[0] != 0)
    def _():
        for i in range(steps):
            arrival(i, 0).start()
            arrival(i, 1).start()
        r_copy.start()

        def take(i):
            arrival(i, 0).wait()
            arrival(i, 1).wait()
            diag[at(i), i * block:] = given[at(i), i * block:].astype(F32)

        def take_r():
            r_copy.wait()
            left_r[...] = r_in[...].astype(F32)

        take(0)
        result = []
        fillers = [functools.partial(take, i) for i in range(1, steps)] + [take_r]
        interleave(root_stages(diag[at(0), at(0)], on_diagonal, identity, result), fillers)
        for k in range(steps):
            root, gap_square = result
            factor_high[at(k), at(k)], factor_low[at(k), at(k)] = root
            near[k:k + 1, :] = jnp.sum(gap_square * gap_square, axis=0, keepdims=True)
            result, part_r = [], []

            def panel(j):
                value = three(nn, root, split(diag[at(k), at(j)]))
                high[:, at(j)], low[:, at(j)] = split(value)
                factor_high[at(j), at(k)], factor_low[at(j), at(k)] = split(value.T)

            def update(i, j):
                left = (factor_high[at(i), at(k)], factor_low[at(i), at(k)])
                diag[at(i), at(j)] -= three(nn, left, (high[:, at(j)], low[:, at(j)]))

            def solve_r():
                part_r.extend(split(three(nt, split(left_r[:, at(k)]), root)))
                solved_r[:, at(k)] = part_r[0]

            def update_r(i):
                left_r[:, at(i)] -= three(nn, part_r, (high[:, at(i)], low[:, at(i)]))

            fillers = [functools.partial(panel, j) for j in range(k + 2, steps)]
            fillers += [
                functools.partial(update, i, j)
                for i in range(k + 1, steps) for j in range(max(i, k + 2), steps)
            ]
            fillers.append(solve_r)
            fillers += [functools.partial(update_r, i) for i in range(k + 1, steps)]
            if k + 1 < steps:
                panel(k + 1)
                update(k + 1, k + 1)
                stages = root_stages(diag[at(k + 1), at(k + 1)], on_diagonal, identity, result)
                interleave(stages, fillers)
            else:
                interleave((), fillers)
        worst = jnp.max(jnp.sum(near[0:steps, :], axis=1, keepdims=True))

        @pl.when(jnp.logical_not(worst <= NEAR**4))
        def _():
            for i in range(steps):
                diag[at(i), i * block:] = given[at(i), i * block:].astype(F32)
            left_r[...] = r_in[...].astype(F32)

            def spot(i):
                return pl.ds(pl.multiple_of(i * block, block), block)

            def eliminate(k, carry):
                now = spot(k)
                root = root_until_near(diag[now, now], on_diagonal, identity, unit_ref, root_ref)
                factor_high[now, now], factor_low[now, now] = root
                part_r = split(three(nt, split(left_r[:, now]), root))
                solved_r[:, now] = part_r[0]

                def panel(j, carry):
                    there = spot(j)
                    value = three(nn, root, split(diag[now, there]))
                    high[:, there], low[:, there] = split(value)
                    factor_high[there, now], factor_low[there, now] = split(value.T)
                    left_r[:, there] -= three(nn, part_r, (high[:, there], low[:, there]))
                    return carry

                def row(i, carry):
                    here = spot(i)
                    left = (factor_high[here, now], factor_low[here, now])

                    def update(j, carry):
                        there = spot(j)
                        diag[here, there] -= three(nn, left, (high[:, there], low[:, there]))
                        return carry

                    return lax.fori_loop(i, steps, update, carry)

                lax.fori_loop(k + 1, steps, panel, 0)
                lax.fori_loop(k + 1, steps, row, 0)
                return carry

            lax.fori_loop(0, steps, eliminate, 0)

        for k in range(steps):
            departure(k, 0).start()
            departure(k, 1).start()
        for k in range(steps):
            departure(k, 0).wait()
            departure(k, 1).wait()


ANY = pl.BlockSpec(memory_space=pl.ANY)
VMEM = pl.BlockSpec(memory_space=pltpu.VMEM)
SMEM = pl.BlockSpec(memory_space=pltpu.SMEM)


def cost(flops, bytes_accessed):
    return pl.CostEstimate(flops=flops, bytes_accessed=bytes_accessed, transcendentals=0)


def params(mib):
    return pltpu.CompilerParams(vmem_limit_bytes=mib * 2**20)


def factor(flags, own_d, other_d, r):
    size, block = own_d.shape[0], BLOCK
    square = jax.ShapeDtypeStruct((size, size), BF16)
    return pl.pallas_call(
        factor_kernel,
        out_shape=(square, square, jax.ShapeDtypeStruct(r.shape, BF16)),
        in_specs=[SMEM, ANY, ANY, ANY],
        out_specs=(ANY, ANY, VMEM),
        scratch_shapes=[
            pltpu.VMEM((size, size), BF16),
            pltpu.VMEM((size, size), F32),
            pltpu.VMEM(r.shape, BF16),
            pltpu.VMEM(r.shape, F32),
            pltpu.VMEM((block, size), BF16),
            pltpu.VMEM((block, size), BF16),
            pltpu.VMEM((size, size), BF16),
            pltpu.VMEM((size, size), BF16),
            pltpu.VMEM((-(-(size // block) // 8) * 8, block), F32),
            pltpu.VMEM((block, block), F32),
            pltpu.VMEM((block, block), F32),
            pltpu.SemaphoreType.DMA((5, size // block)),
        ],
        compiler_params=params(52),
        cost_estimate=cost(18 * 10**9, 16 * 2**20),
    )(flags, own_d, other_d, r)


def fold(first, second, strict):
    rows, columns = strict
    return jnp.where(rows <= columns, first, second), diagonal_row(second, rows == columns)


def unfold(folded, diagonal, strict):
    rows, columns = strict
    turned = folded.T
    first = jnp.where(rows <= columns, folded, turned)
    second = jnp.where(rows > columns, folded, jnp.where(rows < columns, turned, diagonal))
    return first, second


def solve_kernel(flags, high_hbm, low_hbm, e_ref, solved, packed, high, low, rest, turned, sems):
    size, width = e_ref.shape
    block = BLOCK
    steps = size // block
    half = width // 2

    def at(i):
        return slice(i * block, (i + 1) * block)

    def arrival(j, which):
        source, target = ((high_hbm, high), (low_hbm, low))[which]
        columns = slice(0, (j + 1) * block)
        return pltpu.make_async_copy(source.at[at(j), columns], target.at[at(j), columns], sems.at[which, j])

    @pl.when(flags[2] == 0)
    def _():
        solved[...] = jnp.zeros_like(solved)
        packed[...] = jnp.zeros_like(packed)

    @pl.when(flags[2] != 0)
    def _():
        for j in range(steps):
            arrival(j, 0).start()
            arrival(j, 1).start()
        for j in range(steps):
            arrival(j, 0).wait()
            arrival(j, 1).wait()
            root = (high[at(j), at(j)], low[at(j), at(j)])
            if j == 0:
                part = e_ref[at(j), :]
                value = nn(root[0], part) + nn(root[1], part)
            else:
                before = slice(0, j * block)
                left = (high[at(j), before], low[at(j), before])
                part = e_ref[at(j), :].astype(F32) - three(nn, left, (solved[before, :], rest[before, :]))
                value = three(nn, root, split(part))
            solved[at(j), :], rest[at(j), :] = split(value)
            turned[:, at(j)] = value.T.astype(BF16)
        first = nn(turned[0:half, :], solved[:, 0:half])
        second = nn(turned[half:width, :], solved[:, half:width])
        folded, diagonal = fold(first, second, places(half))
        packed[0:half, :] = folded.astype(BF16)
        packed[half:width, :] = nn(turned[0:half, :], solved[:, half:width]).astype(BF16)
        packed[width:, :] = jnp.broadcast_to(diagonal, (16, half)).astype(BF16)


def solve(flags, high, low, e):
    size, width = e.shape
    return pl.pallas_call(
        solve_kernel,
        out_shape=(
            jax.ShapeDtypeStruct(e.shape, BF16),
            jax.ShapeDtypeStruct((width + 16, width // 2), BF16),
        ),
        in_specs=[SMEM, ANY, ANY, VMEM],
        out_specs=(VMEM, VMEM),
        scratch_shapes=[
            pltpu.VMEM((size, size), BF16),
            pltpu.VMEM((size, size), BF16),
            pltpu.VMEM((size, width), BF16),
            pltpu.VMEM((width, size), BF16),
            pltpu.SemaphoreType.DMA((2, size // BLOCK)),
        ],
        compiler_params=params(40),
        cost_estimate=cost(9 * 10**9, 14 * 2**20),
    )(flags, high, low, e)


def tip_kernel(flags, own_r, other_r, out):
    width = own_r.shape[0]

    @pl.when(flags[0] == 0)
    def _():
        out[...] = jnp.zeros_like(out)

    @pl.when(jnp.logical_and(flags[0] != 0, flags[1] == 0))
    def _():
        out[0:width, :] = nt(own_r[...], other_r[...]).astype(BF16)
        out[width:, :] = jnp.zeros((out.shape[0] - width, width), BF16)

    @pl.when(jnp.logical_and(flags[0] != 0, flags[1] != 0))
    def _():
        first = nt(other_r[...], other_r[...])
        second = nt(own_r[...], own_r[...])
        folded, diagonal = fold(first, second, places(width))
        out[0:width, :] = folded.astype(BF16)
        out[width:, :] = jnp.broadcast_to(diagonal, (out.shape[0] - width, width)).astype(BF16)


def tip_term(flags, own_r, other_r):
    width = own_r.shape[0]
    return pl.pallas_call(
        tip_kernel,
        out_shape=jax.ShapeDtypeStruct((width + 64, width), BF16),
        in_specs=[SMEM, VMEM, VMEM],
        out_specs=VMEM,
        compiler_params=params(16),
        cost_estimate=cost(10**9, 3 * 2**20),
    )(flags, own_r, other_r)


def arrow_kernel(flags, own_r, other_r, own_e, out):
    rows = own_r.shape[0]

    @pl.when(flags[2] == 0)
    def _():
        out[...] = jnp.zeros_like(out)

    @pl.when(flags[2] != 0)
    def _():
        core = flags[1]
        for source, side in ((own_r, core), (other_r, 1 - core)):
            place = pl.ds(pl.multiple_of(side * rows, rows), rows)
            out[place, :] = -nn(source[...], own_e[...]).astype(BF16)


def arrow_term(flags, own_r, other_r, own_e):
    return pl.pallas_call(
        arrow_kernel,
        out_shape=jax.ShapeDtypeStruct((2 * own_r.shape[0], own_e.shape[1]), BF16),
        in_specs=[SMEM, VMEM, VMEM, VMEM],
        out_specs=VMEM,
        compiler_params=params(24),
        cost_estimate=cost(2 * 10**9, 6 * 2**20),
    )(flags, own_r, other_r, own_e)


def cross_kernel(flags, own_e, other_e, out):
    width = own_e.shape[1]
    half = width // 2

    @pl.when(flags[2] == 0)
    def _():
        out[...] = jnp.zeros_like(out)

    @pl.when(jnp.logical_and(flags[2] != 0, flags[1] == 0))
    def _():
        out[...] = nn(other_e[:, 0:half].T, own_e[...]).astype(BF16)

    @pl.when(jnp.logical_and(flags[2] != 0, flags[1] != 0))
    def _():
        out[...] = nn(own_e[:, half:width].T, other_e[...]).astype(BF16)


def cross_term(flags, own_e, other_e):
    width = own_e.shape[1]
    return pl.pallas_call(
        cross_kernel,
        out_shape=jax.ShapeDtypeStruct((width // 2, width), BF16),
        in_specs=[SMEM, VMEM, VMEM],
        out_specs=VMEM,
        compiler_params=params(24),
        cost_estimate=cost(2 * 10**9, 6 * 2**20),
    )(flags, own_e, other_e)


def separator_kernel(flags, separator, packed, own_cross, other_cross, out):
    width = separator.shape[1]
    half = width // 2
    core = flags[1]
    first, second = unfold(
        packed[0:half, :].astype(F32), packed[width:width + 1, :].astype(F32), places(half)
    )
    corner = packed[half:width, :].astype(F32)
    base = pl.multiple_of(core * width, width)

    def less(rows, columns, term):
        out[rows, columns] = (separator[rows, columns].astype(F32) - term).astype(BF16)

    top, bottom = pl.ds(base, half), pl.ds(base + half, half)
    left, right = slice(0, half), slice(half, width)
    less(top, left, first)
    less(top, right, corner)
    less(bottom, left, corner.T)
    less(bottom, right, second)

    @pl.when(core == 0)
    def _():
        less(slice(width, width + half), slice(0, width), own_cross[...].astype(F32))
        less(slice(width + half, 2 * width), slice(0, width), other_cross[...].astype(F32))

    @pl.when(core != 0)
    def _():
        less(slice(0, width), left, other_cross[...].astype(F32).T)
        less(slice(0, width), right, own_cross[...].astype(F32).T)


def separator_less(flags, separator, packed, own_cross, other_cross):
    return pl.pallas_call(
        separator_kernel,
        out_shape=jax.ShapeDtypeStruct(separator.shape, BF16),
        in_specs=[SMEM, VMEM, VMEM, VMEM, VMEM],
        out_specs=VMEM,
        compiler_params=params(24),
        cost_estimate=cost(10**6, 6 * 2**20),
    )(flags, separator, packed, own_cross, other_cross)


def new_tip_kernel(flags, tip, own_sum, other_sum, out):
    width = tip.shape[1]
    core = flags[1]

    @pl.when(core == 0)
    def _():
        first, _ = unfold(
            other_sum[0:width, :].astype(F32), other_sum[width:width + 1, :].astype(F32), places(width)
        )
        out[0:width, :] = tip[0:width, :].astype(F32) - first
        out[width:, :] = tip[width:, :].astype(F32) - own_sum[0:width, :].astype(F32).T

    @pl.when(core != 0)
    def _():
        _, second = unfold(
            own_sum[0:width, :].astype(F32), own_sum[width:width + 1, :].astype(F32), places(width)
        )
        out[0:width, :] = tip[0:width, :].astype(F32) - other_sum[0:width, :].astype(F32)
        out[width:, :] = tip[width:, :].astype(F32) - second


def tip_less(flags, tip, own_sum, other_sum):
    return pl.pallas_call(
        new_tip_kernel,
        out_shape=jax.ShapeDtypeStruct(tip.shape, F32),
        in_specs=[SMEM, VMEM, VMEM, VMEM],
        out_specs=VMEM,
        compiler_params=params(16),
        cost_estimate=cost(10**6, 3 * 2**20),
    )(flags, tip, own_sum, other_sum)


def swapped(x):
    return lax.ppermute(x, "space", [(0, 1), (1, 0)])


def to_previous(x):
    count = lax.axis_size("tm")
    return lax.ppermute(x, "tm", [(i, i - 1) for i in range(1, count)])


def exchanged(x, distance):
    return lax.ppermute(x, "tm", [(i, i ^ distance) for i in range(lax.axis_size("tm"))])


def kept_and_sent(x, upper):
    half = x.shape[0] // 2
    low, high = x[:half], x[half:]
    return jnp.where(upper, high, low), jnp.where(upper, low, high)


def summed(x):
    count = lax.axis_size("tm")
    position = lax.axis_index("tm")
    far = [1 << i for i in range(1, count.bit_length() - 1)]
    halving = far[:2]
    for distance in halving:
        kept, sent = kept_and_sent(x, (position & distance) != 0)
        x = (kept.astype(F32) + exchanged(sent, distance).astype(F32)).astype(BF16)
    for distance in far[2:] + [1]:
        x = (x.astype(F32) + exchanged(x, distance).astype(F32)).astype(BF16)
    for distance in reversed(halving):
        other = exchanged(x, distance)
        upper = (position & distance) != 0
        x = jnp.concatenate([jnp.where(upper, other, x), jnp.where(upper, x, other)], axis=0)
    return x


def on_device(interior_diag, coupling, arrow_rows, separator_diag, tip, lengths):
    position = lax.axis_index("tm")
    active = lengths[position] == 2
    flags = jnp.stack(
        [active, lax.axis_index("space") != 0, jnp.logical_and(active, position != 0)]
    ).astype(jnp.int32)
    other_diag = swapped(interior_diag)
    high, low, own_r = factor(flags, interior_diag, other_diag, arrow_rows)
    other_r = swapped(own_r)
    own_e, packed = solve(flags, high, low, coupling)
    packed = to_previous(packed)
    other_e = swapped(own_e)
    tip_sum = summed(tip_term(flags, own_r, other_r))
    cross = to_previous(cross_term(flags, own_e, other_e))
    arrow_fill = to_previous(arrow_term(flags, own_r, other_r, own_e))
    new_separator = separator_less(flags, separator_diag, packed, cross, swapped(cross))
    new_tip = tip_less(flags, tip, tip_sum, swapped(tip_sum))
    return (new_separator, arrow_fill, new_tip)


def solution(mesh):
    return jax.shard_map(
        on_device,
        mesh=mesh,
        in_specs=(
            P(("groups", "tm"), "space"),
            P(("groups", "tm"), "space"),
            P(("groups", "tm", "space"), None),
            P(("groups", "tm"), "space"),
            P("groups", "space"),
            P("groups"),
        ),
        out_specs=(
            P(("groups", "tm"), "space"),
            P(("groups", "tm"), "space"),
            P("groups", "space"),
        ),
        check_vma=False,
    )
```

```python
import functools

import jax
import jax.numpy as jnp
from jax import lax
from jax.experimental import pallas as pl
from jax.experimental.pallas import tpu as pltpu
from jax.sharding import PartitionSpec as P

F32 = jnp.float32
BF16 = jnp.bfloat16
BLOCK = 256
NEAR = 0.03
MOST_STEPS = 60
STAGES = 7


def split(x):
    high = x.astype(BF16)
    return high, (x - high.astype(F32)).astype(BF16)


def nn(a, b):
    return lax.dot_general(a, b, (((1,), (0,)), ((), ())), preferred_element_type=F32)


def nt(a, b):
    return lax.dot_general(a, b, (((1,), (1,)), ((), ())), preferred_element_type=F32)


def three(dot, a, b):
    return dot(a[0], b[0]) + (dot(a[0], b[1]) + dot(a[1], b[0]))


def total(x):
    return jnp.sum(x, keepdims=True)


def places(size):
    rows = lax.broadcasted_iota(jnp.int32, (size, size), 0)
    columns = lax.broadcasted_iota(jnp.int32, (size, size), 1)
    return rows, columns


def diagonal_row(x, on_diagonal):
    return jnp.sum(jnp.where(on_diagonal, x, 0.0), axis=0, keepdims=True)


def unit_scaled(a, on_diagonal):
    diagonal = jnp.where(on_diagonal, a, 0.0)
    scale_row = lax.rsqrt(jnp.sum(diagonal, axis=0, keepdims=True))
    scale_column = lax.rsqrt(jnp.sum(diagonal, axis=1, keepdims=True))
    return a * scale_row * scale_column, scale_row


def first_root(off, off_square, identity):
    bound = jnp.sqrt(jnp.sqrt(total(off_square * off_square)))
    c = jnp.minimum(1.0, 1.9 / (1.0 + bound))
    gap = c * off - (1.0 - c) * identity
    gap_square = c * c * off_square - (2 * c * (1 - c)) * off + ((1 - c) * (1 - c)) * identity
    return (jnp.sqrt(c) * (identity - 0.5 * gap + 0.375 * gap_square)).astype(BF16)


def root_stages(a, on_diagonal, identity, result):
    unit, scale_row = unit_scaled(a, on_diagonal)
    off = unit - identity
    off_high = off.astype(BF16)
    high, low = split(unit)
    yield
    off_square = nn(off_high, off_high)
    yield
    first = first_root(off, off_square, identity)
    yield
    product = split(nt(high, first) + nt(low, first))
    yield
    gap = nn(first, product[0]) + nn(first, product[1]) - identity
    gap_high = gap.astype(BF16)
    yield
    gap_square = nn(gap_high, gap_high)
    change = split(0.375 * gap_square - 0.5 * gap)
    yield
    root = first.astype(F32) + (nn(change[0], first) + nn(change[1], first))
    result.append(split(root * scale_row))
    result.append(gap_square)


def root_until_near(a, on_diagonal, identity, unit_ref, root_ref):
    unit, scale_row = unit_scaled(a, on_diagonal)
    off = unit - identity
    off_square = nn(off.astype(BF16), off.astype(BF16))
    unit_ref[...] = unit
    root_ref[...] = first_root(off, off_square, identity).astype(F32)

    def far(state):
        return jnp.logical_and(jnp.logical_not(state[0] <= NEAR**4), state[1] < MOST_STEPS)

    def step(state):
        root = split(root_ref[...])
        product = split(three(nt, split(unit_ref[...]), root))
        gap = three(nn, root, product) - identity
        gap_square = nn(gap.astype(BF16), gap.astype(BF16))
        change = split(0.375 * gap_square - 0.5 * gap)
        root_ref[...] += three(nn, change, root)
        return jnp.sum(gap_square * gap_square), state[1] + 1

    lax.while_loop(far, step, (jnp.float32(1.0), jnp.int32(0)))
    return split(root_ref[...] * scale_row)


def interleave(stages, fillers):
    share = -(-len(fillers) // STAGES)
    for _ in stages:
        for filler in fillers[:share]:
            filler()
        fillers = fillers[share:]
    for filler in fillers:
        filler()


def eliminate_kernel(
    flags, own_d, other_d, e_hbm, r_hbm, solved_e, solved_r, packed,
    given, diag, e_in, r_in, left_r, high, low, factor_high, factor_low, rest_e, turned,
    near, unit_ref, root_ref, sems,
):
    size, block = diag.shape[0], unit_ref.shape[0]
    half, width = own_d.shape[1], e_in.shape[1]
    steps = size // block
    core = flags[1]

    def at(i):
        return slice(i * block, (i + 1) * block)

    def arrival(i, which):
        source = own_d if which == 0 else other_d
        side = core if which == 0 else 1 - core
        columns = pl.ds(pl.multiple_of(side * half, half), half)
        return pltpu.make_async_copy(source.at[at(i), :], given.at[at(i), columns], sems.at[which, i])

    rows, columns = places(block)
    on_diagonal = rows == columns
    identity = jnp.where(on_diagonal, 1.0, 0.0).astype(F32)
    e_copy = pltpu.make_async_copy(e_hbm, e_in, sems.at[2, 0])
    r_copy = pltpu.make_async_copy(r_hbm, r_in, sems.at[2, 1])

    def solve_e(k, root):
        part = e_in[at(k), :]
        if k == 0:
            value = nn(root[0], part) + nn(root[1], part)
        else:
            before = slice(0, k * block)
            left = (factor_high[at(k), before], factor_low[at(k), before])
            part = part.astype(F32) - three(nn, left, (solved_e[before, :], rest_e[before, :]))
            value = three(nn, root, split(part))
        solved_e[at(k), :], rest_e[at(k), :] = split(value)
        turned[:, at(k)] = value.T.astype(BF16)

    @pl.when(flags[0] == 0)
    def _():
        solved_e[...] = jnp.zeros_like(solved_e)
        solved_r[...] = jnp.zeros_like(solved_r)
        packed[...] = jnp.zeros_like(packed)

    @pl.when(flags[0] != 0)
    def _():
        for i in range(steps):
            arrival(i, 0).start()
            arrival(i, 1).start()
        r_copy.start()
        e_copy.start()

        def take(i):
            arrival(i, 0).wait()
            arrival(i, 1).wait()
            diag[at(i), i * block:] = given[at(i), i * block:].astype(F32)

        def take_r():
            r_copy.wait()
            left_r[...] = r_in[...].astype(F32)

        take(0)
        result = []
        fillers = [functools.partial(take, i) for i in range(1, steps)] + [take_r, e_copy.wait]
        interleave(root_stages(diag[at(0), at(0)], on_diagonal, identity, result), fillers)
        for k in range(steps):
            root, gap_square = result
            near[k:k + 1, :] = jnp.sum(gap_square * gap_square, axis=0, keepdims=True)
            result, part_r = [], []

            def panel(j):
                value = three(nn, root, split(diag[at(k), at(j)]))
                high[:, at(j)], low[:, at(j)] = split(value)
                factor_high[at(j), at(k)], factor_low[at(j), at(k)] = split(value.T)

            def update(i, j):
                left = (factor_high[at(i), at(k)], factor_low[at(i), at(k)])
                diag[at(i), at(j)] -= three(nn, left, (high[:, at(j)], low[:, at(j)]))

            def solve_r():
                part_r.extend(split(three(nt, split(left_r[:, at(k)]), root)))
                solved_r[:, at(k)] = part_r[0]

            def update_r(i):
                left_r[:, at(i)] -= three(nn, part_r, (high[:, at(i)], low[:, at(i)]))

            fillers = [functools.partial(panel, j) for j in range(k + 2, steps)]
            fillers += [
                functools.partial(update, i, j)
                for i in range(k + 1, steps) for j in range(max(i, k + 2), steps)
            ]
            fillers.append(solve_r)
            fillers += [functools.partial(update_r, i) for i in range(k + 1, steps)]
            fillers.append(functools.partial(solve_e, k, root))
            if k + 1 < steps:
                panel(k + 1)
                update(k + 1, k + 1)
                stages = root_stages(diag[at(k + 1), at(k + 1)], on_diagonal, identity, result)
                interleave(stages, fillers)
            else:
                interleave((), fillers)
        worst = jnp.max(jnp.sum(near[0:steps, :], axis=1, keepdims=True))

        @pl.when(jnp.logical_not(worst <= NEAR**4))
        def _():
            for i in range(steps):
                diag[at(i), i * block:] = given[at(i), i * block:].astype(F32)
            left_r[...] = r_in[...].astype(F32)

            def spot(i):
                return pl.ds(pl.multiple_of(i * block, block), block)

            def eliminate(k, carry):
                now = spot(k)
                root = root_until_near(diag[now, now], on_diagonal, identity, unit_ref, root_ref)
                part_r = split(three(nt, split(left_r[:, now]), root))
                solved_r[:, now] = part_r[0]

                def left_of(j, part):
                    there = spot(j)
                    left = (factor_high[now, there], factor_low[now, there])
                    return part - three(nn, left, (solved_e[there, :], rest_e[there, :]))

                part_e = lax.fori_loop(0, k, left_of, e_in[now, :].astype(F32))
                value = three(nn, root, split(part_e))
                solved_e[now, :], rest_e[now, :] = split(value)
                turned[:, now] = value.T.astype(BF16)

                def panel(j, carry):
                    there = spot(j)
                    value = three(nn, root, split(diag[now, there]))
                    high[:, there], low[:, there] = split(value)
                    factor_high[there, now], factor_low[there, now] = split(value.T)
                    left_r[:, there] -= three(nn, part_r, (high[:, there], low[:, there]))
                    return carry

                def row(i, carry):
                    here = spot(i)
                    left = (factor_high[here, now], factor_low[here, now])

                    def update(j, carry):
                        there = spot(j)
                        diag[here, there] -= three(nn, left, (high[:, there], low[:, there]))
                        return carry

                    return lax.fori_loop(i, steps, update, carry)

                lax.fori_loop(k + 1, steps, panel, 0)
                lax.fori_loop(k + 1, steps, row, 0)
                return carry

            lax.fori_loop(0, steps, eliminate, 0)

        corner = width // 2
        first = nn(turned[0:corner, :], solved_e[:, 0:corner])
        second = nn(turned[corner:width, :], solved_e[:, corner:width])
        folded, diagonal = fold(first, second, places(corner))
        packed[0:corner, :] = folded.astype(BF16)
        packed[corner:width, :] = nn(turned[0:corner, :], solved_e[:, corner:width]).astype(BF16)
        packed[width:, :] = jnp.broadcast_to(diagonal, (16, corner)).astype(BF16)


def fold(first, second, strict):
    rows, columns = strict
    return jnp.where(rows <= columns, first, second), diagonal_row(second, rows == columns)


def unfold(folded, diagonal, strict):
    rows, columns = strict
    turned = folded.T
    first = jnp.where(rows <= columns, folded, turned)
    second = jnp.where(rows > columns, folded, jnp.where(rows < columns, turned, diagonal))
    return first, second


ANY = pl.BlockSpec(memory_space=pl.ANY)
VMEM = pl.BlockSpec(memory_space=pltpu.VMEM)
SMEM = pl.BlockSpec(memory_space=pltpu.SMEM)


def cost(flops, bytes_accessed):
    return pl.CostEstimate(flops=flops, bytes_accessed=bytes_accessed, transcendentals=0)


def params(mib):
    return pltpu.CompilerParams(vmem_limit_bytes=mib * 2**20)


def eliminate(flags, own_d, other_d, e, r):
    size, block = own_d.shape[0], BLOCK
    width = e.shape[1]
    return pl.pallas_call(
        eliminate_kernel,
        out_shape=(
            jax.ShapeDtypeStruct(e.shape, BF16),
            jax.ShapeDtypeStruct(r.shape, BF16),
            jax.ShapeDtypeStruct((width + 16, width // 2), BF16),
        ),
        in_specs=[SMEM, ANY, VMEM, ANY, ANY],
        out_specs=(VMEM, VMEM, VMEM),
        scratch_shapes=[
            pltpu.VMEM((size, size), BF16),
            pltpu.VMEM((size, size), F32),
            pltpu.VMEM(e.shape, BF16),
            pltpu.VMEM(r.shape, BF16),
            pltpu.VMEM(r.shape, F32),
            pltpu.VMEM((block, size), BF16),
            pltpu.VMEM((block, size), BF16),
            pltpu.VMEM((size, size), BF16),
            pltpu.VMEM((size, size), BF16),
            pltpu.VMEM(e.shape, BF16),
            pltpu.VMEM((width, size), BF16),
            pltpu.VMEM((-(-(size // block) // 8) * 8, block), F32),
            pltpu.VMEM((block, block), F32),
            pltpu.VMEM((block, block), F32),
            pltpu.SemaphoreType.DMA((3, size // block)),
        ],
        compiler_params=params(52),
        cost_estimate=cost(28 * 10**9, 16 * 2**20),
    )(flags, own_d, other_d, e, r)


def tip_kernel(flags, own_r, other_r, out):
    width = own_r.shape[0]

    @pl.when(flags[0] == 0)
    def _():
        out[...] = jnp.zeros_like(out)

    @pl.when(jnp.logical_and(flags[0] != 0, flags[1] == 0))
    def _():
        out[0:width, :] = nt(own_r[...], other_r[...]).astype(BF16)
        out[width:, :] = jnp.zeros((out.shape[0] - width, width), BF16)

    @pl.when(jnp.logical_and(flags[0] != 0, flags[1] != 0))
    def _():
        first = nt(other_r[...], other_r[...])
        second = nt(own_r[...], own_r[...])
        folded, diagonal = fold(first, second, places(width))
        out[0:width, :] = folded.astype(BF16)
        out[width:, :] = jnp.broadcast_to(diagonal, (out.shape[0] - width, width)).astype(BF16)


def tip_term(flags, own_r, other_r):
    width = own_r.shape[0]
    return pl.pallas_call(
        tip_kernel,
        out_shape=jax.ShapeDtypeStruct((width + 64, width), BF16),
        in_specs=[SMEM, VMEM, VMEM],
        out_specs=VMEM,
        compiler_params=params(16),
        cost_estimate=cost(10**9, 3 * 2**20),
    )(flags, own_r, other_r)


def arrow_kernel(flags, own_r, other_r, own_e, out):
    rows = own_r.shape[0]

    @pl.when(flags[2] == 0)
    def _():
        out[...] = jnp.zeros_like(out)

    @pl.when(flags[2] != 0)
    def _():
        core = flags[1]
        for source, side in ((own_r, core), (other_r, 1 - core)):
            place = pl.ds(pl.multiple_of(side * rows, rows), rows)
            out[place, :] = -nn(source[...], own_e[...]).astype(BF16)


def arrow_term(flags, own_r, other_r, own_e):
    return pl.pallas_call(
        arrow_kernel,
        out_shape=jax.ShapeDtypeStruct((2 * own_r.shape[0], own_e.shape[1]), BF16),
        in_specs=[SMEM, VMEM, VMEM, VMEM],
        out_specs=VMEM,
        compiler_params=params(24),
        cost_estimate=cost(2 * 10**9, 6 * 2**20),
    )(flags, own_r, other_r, own_e)


def cross_kernel(flags, own_e, other_e, out):
    width = own_e.shape[1]
    half = width // 2

    @pl.when(flags[2] == 0)
    def _():
        out[...] = jnp.zeros_like(out)

    @pl.when(jnp.logical_and(flags[2] != 0, flags[1] == 0))
    def _():
        out[...] = nn(other_e[:, 0:half].T, own_e[...]).astype(BF16)

    @pl.when(jnp.logical_and(flags[2] != 0, flags[1] != 0))
    def _():
        out[...] = nn(own_e[:, half:width].T, other_e[...]).astype(BF16)


def cross_term(flags, own_e, other_e):
    width = own_e.shape[1]
    return pl.pallas_call(
        cross_kernel,
        out_shape=jax.ShapeDtypeStruct((width // 2, width), BF16),
        in_specs=[SMEM, VMEM, VMEM],
        out_specs=VMEM,
        compiler_params=params(24),
        cost_estimate=cost(2 * 10**9, 6 * 2**20),
    )(flags, own_e, other_e)


def separator_kernel(flags, separator, packed, own_cross, other_cross, out):
    width = separator.shape[1]
    half = width // 2
    core = flags[1]
    first, second = unfold(
        packed[0:half, :].astype(F32), packed[width:width + 1, :].astype(F32), places(half)
    )
    corner = packed[half:width, :].astype(F32)
    base = pl.multiple_of(core * width, width)

    def less(rows, columns, term):
        out[rows, columns] = (separator[rows, columns].astype(F32) - term).astype(BF16)

    top, bottom = pl.ds(base, half), pl.ds(base + half, half)
    left, right = slice(0, half), slice(half, width)
    less(top, left, first)
    less(top, right, corner)
    less(bottom, left, corner.T)
    less(bottom, right, second)

    @pl.when(core == 0)
    def _():
        less(slice(width, width + half), slice(0, width), own_cross[...].astype(F32))
        less(slice(width + half, 2 * width), slice(0, width), other_cross[...].astype(F32))

    @pl.when(core != 0)
    def _():
        less(slice(0, width), left, other_cross[...].astype(F32).T)
        less(slice(0, width), right, own_cross[...].astype(F32).T)


def separator_less(flags, separator, packed, own_cross, other_cross):
    return pl.pallas_call(
        separator_kernel,
        out_shape=jax.ShapeDtypeStruct(separator.shape, BF16),
        in_specs=[SMEM, VMEM, VMEM, VMEM, VMEM],
        out_specs=VMEM,
        compiler_params=params(24),
        cost_estimate=cost(10**6, 6 * 2**20),
    )(flags, separator, packed, own_cross, other_cross)


def new_tip_kernel(flags, tip, own_sum, other_sum, out):
    width = tip.shape[1]
    core = flags[1]

    @pl.when(core == 0)
    def _():
        first, _ = unfold(
            other_sum[0:width, :].astype(F32), other_sum[width:width + 1, :].astype(F32), places(width)
        )
        out[0:width, :] = tip[0:width, :].astype(F32) - first
        out[width:, :] = tip[width:, :].astype(F32) - own_sum[0:width, :].astype(F32).T

    @pl.when(core != 0)
    def _():
        _, second = unfold(
            own_sum[0:width, :].astype(F32), own_sum[width:width + 1, :].astype(F32), places(width)
        )
        out[0:width, :] = tip[0:width, :].astype(F32) - other_sum[0:width, :].astype(F32)
        out[width:, :] = tip[width:, :].astype(F32) - second


def tip_less(flags, tip, own_sum, other_sum):
    return pl.pallas_call(
        new_tip_kernel,
        out_shape=jax.ShapeDtypeStruct(tip.shape, F32),
        in_specs=[SMEM, VMEM, VMEM, VMEM],
        out_specs=VMEM,
        compiler_params=params(16),
        cost_estimate=cost(10**6, 3 * 2**20),
    )(flags, tip, own_sum, other_sum)


def swapped(x):
    return lax.ppermute(x, "space", [(0, 1), (1, 0)])


def to_previous(x):
    count = lax.axis_size("tm")
    return lax.ppermute(x, "tm", [(i, i - 1) for i in range(1, count)])


def exchanged(x, distance):
    return lax.ppermute(x, "tm", [(i, i ^ distance) for i in range(lax.axis_size("tm"))])


def kept_and_sent(x, upper):
    half = x.shape[0] // 2
    low, high = x[:half], x[half:]
    return jnp.where(upper, high, low), jnp.where(upper, low, high)


def summed(x):
    count = lax.axis_size("tm")
    position = lax.axis_index("tm")
    far = [1 << i for i in range(1, count.bit_length() - 1)]
    halving = far[:2]
    for distance in halving:
        kept, sent = kept_and_sent(x, (position & distance) != 0)
        x = (kept.astype(F32) + exchanged(sent, distance).astype(F32)).astype(BF16)
    for distance in far[2:] + [1]:
        x = (x.astype(F32) + exchanged(x, distance).astype(F32)).astype(BF16)
    for distance in reversed(halving):
        other = exchanged(x, distance)
        upper = (position & distance) != 0
        x = jnp.concatenate([jnp.where(upper, other, x), jnp.where(upper, x, other)], axis=0)
    return x


def on_device(interior_diag, coupling, arrow_rows, separator_diag, tip, lengths):
    position = lax.axis_index("tm")
    active = lengths[position] == 2
    flags = jnp.stack(
        [active, lax.axis_index("space") != 0, jnp.logical_and(active, position != 0)]
    ).astype(jnp.int32)
    other_diag = swapped(interior_diag)
    own_e, own_r, packed = eliminate(flags, interior_diag, other_diag, coupling, arrow_rows)
    packed = to_previous(packed)
    other_e = swapped(own_e)
    other_r = swapped(own_r)
    cross = cross_term(flags, own_e, other_e)
    cross = to_previous(cross)
    arrow = arrow_term(flags, own_r, other_r, own_e)
    arrow_fill = to_previous(arrow)
    term = tip_term(flags, own_r, other_r)
    tip_sum = summed(term)
    other_cross = swapped(cross)
    new_separator = separator_less(flags, separator_diag, packed, cross, other_cross)
    other_sum = swapped(tip_sum)
    new_tip = tip_less(flags, tip, tip_sum, other_sum)
    return (new_separator, arrow_fill, new_tip)


def solution(mesh):
    return jax.shard_map(
        on_device,
        mesh=mesh,
        in_specs=(
            P(("groups", "tm"), "space"),
            P(("groups", "tm"), "space"),
            P(("groups", "tm", "space"), None),
            P(("groups", "tm"), "space"),
            P("groups", "space"),
            P("groups"),
        ),
        out_specs=(
            P(("groups", "tm"), "space"),
            P(("groups", "tm"), "space"),
            P("groups", "space"),
        ),
        check_vma=False,
    )
```

```python
import functools

import jax
import jax.numpy as jnp
from jax import lax
from jax.experimental import pallas as pl
from jax.experimental.pallas import tpu as pltpu
from jax.sharding import PartitionSpec as P


F32 = jnp.float32
BF16 = jnp.bfloat16
BLOCK = 256
NEAR = 0.03
MOST_STEPS = 60
STAGES = 7
PAD = 16
PIECES = 3
SHARDS = 4


def split(x):
    high = x.astype(BF16)
    return high, (x - high.astype(F32)).astype(BF16)


def nn(a, b):
    return lax.dot_general(a, b, (((1,), (0,)), ((), ())), preferred_element_type=F32)


def nt(a, b):
    return lax.dot_general(a, b, (((1,), (1,)), ((), ())), preferred_element_type=F32)


def three(dot, a, b):
    return dot(a[0], b[0]) + (dot(a[0], b[1]) + dot(a[1], b[0]))


def total(x):
    return jnp.sum(x, keepdims=True)


def places(size):
    rows = lax.broadcasted_iota(jnp.int32, (size, size), 0)
    columns = lax.broadcasted_iota(jnp.int32, (size, size), 1)
    return rows, columns


def diagonal_row(x, on_diagonal):
    return jnp.sum(jnp.where(on_diagonal, x, 0.0), axis=0, keepdims=True)


def unit_scaled(a, on_diagonal):
    diagonal = jnp.where(on_diagonal, a, 0.0)
    scale_row = lax.rsqrt(jnp.sum(diagonal, axis=0, keepdims=True))
    scale_column = lax.rsqrt(jnp.sum(diagonal, axis=1, keepdims=True))
    return a * scale_row * scale_column, scale_row


def first_root(off, off_square, identity):
    bound = jnp.sqrt(jnp.sqrt(total(off_square * off_square)))
    c = jnp.minimum(1.0, 1.9 / (1.0 + bound))
    gap = c * off - (1.0 - c) * identity
    gap_square = c * c * off_square - (2 * c * (1 - c)) * off + ((1 - c) * (1 - c)) * identity
    return (jnp.sqrt(c) * (identity - 0.5 * gap + 0.375 * gap_square)).astype(BF16)


def root_stages(a, on_diagonal, identity, result):
    unit, scale_row = unit_scaled(a, on_diagonal)
    off = unit - identity
    off_high = off.astype(BF16)
    high, low = split(unit)
    yield
    off_square = nn(off_high, off_high)
    yield
    first = first_root(off, off_square, identity)
    yield
    product = split(nt(high, first) + nt(low, first))
    yield
    gap = nn(first, product[0]) + nn(first, product[1]) - identity
    gap_high = gap.astype(BF16)
    yield
    gap_square = nn(gap_high, gap_high)
    change = split(0.375 * gap_square - 0.5 * gap)
    yield
    root = first.astype(F32) + (nn(change[0], first) + nn(change[1], first))
    result.append(split(root * scale_row))
    result.append(gap_square)


def root_until_near(a, on_diagonal, identity, unit_ref, root_ref):
    unit, scale_row = unit_scaled(a, on_diagonal)
    off = unit - identity
    off_square = nn(off.astype(BF16), off.astype(BF16))
    unit_ref[...] = unit
    root_ref[...] = first_root(off, off_square, identity).astype(F32)

    def far(state):
        return jnp.logical_and(jnp.logical_not(state[0] <= NEAR**4), state[1] < MOST_STEPS)

    def step(state):
        root = split(root_ref[...])
        product = split(three(nt, split(unit_ref[...]), root))
        gap = three(nn, root, product) - identity
        gap_square = nn(gap.astype(BF16), gap.astype(BF16))
        change = split(0.375 * gap_square - 0.5 * gap)
        root_ref[...] += three(nn, change, root)
        return jnp.sum(gap_square * gap_square), state[1] + 1

    lax.while_loop(far, step, (jnp.float32(1.0), jnp.int32(0)))
    return split(root_ref[...] * scale_row)


def interleave(stages, fillers):
    share = -(-len(fillers) // STAGES)
    for _ in stages:
        for filler in fillers[:share]:
            filler()
        fillers = fillers[share:]
    for filler in fillers:
        filler()


def eliminate_kernel(
    flags, own_d, other_d, e_hbm, r_hbm, solved_e, solved_r, corner_out, folded_out,
    given, diag, e_in, r_in, left_r, high, low, factor_high, factor_low, rest_e, turned,
    near, unit_ref, root_ref, sems,
):
    size, block = diag.shape[0], unit_ref.shape[0]
    half, width = own_d.shape[1], e_in.shape[1]
    steps = size // block
    core = flags[1]

    def at(i):
        return slice(i * block, (i + 1) * block)

    def arrival(i, which):
        source = own_d if which == 0 else other_d
        side = core if which == 0 else 1 - core
        columns = pl.ds(pl.multiple_of(side * half, half), half)
        return pltpu.make_async_copy(source.at[at(i), :], given.at[at(i), columns], sems.at[which, i])

    rows, columns = places(block)
    on_diagonal = rows == columns
    identity = jnp.where(on_diagonal, 1.0, 0.0).astype(F32)
    e_copy = pltpu.make_async_copy(e_hbm, e_in, sems.at[2, 0])
    r_copy = pltpu.make_async_copy(r_hbm, r_in, sems.at[2, 1])

    def solve_e(k, root):
        part = e_in[at(k), :]
        if k == 0:
            value = nn(root[0], part) + nn(root[1], part)
        else:
            before = slice(0, k * block)
            left = (factor_high[at(k), before], factor_low[at(k), before])
            part = part.astype(F32) - three(nn, left, (solved_e[before, :], rest_e[before, :]))
            value = three(nn, root, split(part))
        solved_e[at(k), :], rest_e[at(k), :] = split(value)
        turned[:, at(k)] = value.T.astype(BF16)

    @pl.when(flags[0] == 0)
    def _():
        solved_e[...] = jnp.zeros_like(solved_e)
        solved_r[...] = jnp.zeros_like(solved_r)
        corner_out[...] = jnp.zeros_like(corner_out)
        folded_out[...] = jnp.zeros_like(folded_out)

    @pl.when(flags[0] != 0)
    def _():
        for i in range(steps):
            arrival(i, 0).start()
            arrival(i, 1).start()
        r_copy.start()
        e_copy.start()

        def take(i):
            arrival(i, 0).wait()
            arrival(i, 1).wait()
            diag[at(i), i * block:] = given[at(i), i * block:].astype(F32)

        def take_r():
            r_copy.wait()
            left_r[...] = r_in[...].astype(F32)

        take(0)
        result = []
        fillers = [functools.partial(take, i) for i in range(1, steps)] + [take_r, e_copy.wait]
        interleave(root_stages(diag[at(0), at(0)], on_diagonal, identity, result), fillers)
        for k in range(steps):
            root, gap_square = result
            near[k:k + 1, :] = jnp.sum(gap_square * gap_square, axis=0, keepdims=True)
            result, part_r = [], []

            def panel(j):
                value = three(nn, root, split(diag[at(k), at(j)]))
                high[:, at(j)], low[:, at(j)] = split(value)
                factor_high[at(j), at(k)], factor_low[at(j), at(k)] = split(value.T)

            def update(i, j):
                left = (factor_high[at(i), at(k)], factor_low[at(i), at(k)])
                diag[at(i), at(j)] -= three(nn, left, (high[:, at(j)], low[:, at(j)]))

            def solve_r():
                part_r.extend(split(three(nt, split(left_r[:, at(k)]), root)))
                solved_r[:, at(k)] = part_r[0]

            def update_r(i):
                left_r[:, at(i)] -= three(nn, part_r, (high[:, at(i)], low[:, at(i)]))

            fillers = [functools.partial(panel, j) for j in range(k + 2, steps)]
            fillers += [
                functools.partial(update, i, j)
                for i in range(k + 1, steps) for j in range(max(i, k + 2), steps)
            ]
            fillers.append(solve_r)
            fillers += [functools.partial(update_r, i) for i in range(k + 1, steps)]
            fillers.append(functools.partial(solve_e, k, root))
            if k + 1 < steps:
                panel(k + 1)
                update(k + 1, k + 1)
                stages = root_stages(diag[at(k + 1), at(k + 1)], on_diagonal, identity, result)
                interleave(stages, fillers)
            else:
                interleave((), fillers)
        worst = jnp.max(jnp.sum(near[0:steps, :], axis=1, keepdims=True))

        @pl.when(jnp.logical_not(worst <= NEAR**4))
        def _():
            for i in range(steps):
                diag[at(i), i * block:] = given[at(i), i * block:].astype(F32)
            left_r[...] = r_in[...].astype(F32)

            def spot(i):
                return pl.ds(pl.multiple_of(i * block, block), block)

            def eliminate(k, carry):
                now = spot(k)
                root = root_until_near(diag[now, now], on_diagonal, identity, unit_ref, root_ref)
                part_r = split(three(nt, split(left_r[:, now]), root))
                solved_r[:, now] = part_r[0]

                def left_of(j, part):
                    there = spot(j)
                    left = (factor_high[now, there], factor_low[now, there])
                    return part - three(nn, left, (solved_e[there, :], rest_e[there, :]))

                part_e = lax.fori_loop(0, k, left_of, e_in[now, :].astype(F32))
                value = three(nn, root, split(part_e))
                solved_e[now, :], rest_e[now, :] = split(value)
                turned[:, now] = value.T.astype(BF16)

                def panel(j, carry):
                    there = spot(j)
                    value = three(nn, root, split(diag[now, there]))
                    high[:, there], low[:, there] = split(value)
                    factor_high[there, now], factor_low[there, now] = split(value.T)
                    left_r[:, there] -= three(nn, part_r, (high[:, there], low[:, there]))
                    return carry

                def row(i, carry):
                    here = spot(i)
                    left = (factor_high[here, now], factor_low[here, now])

                    def update(j, carry):
                        there = spot(j)
                        diag[here, there] -= three(nn, left, (high[:, there], low[:, there]))
                        return carry

                    return lax.fori_loop(i, steps, update, carry)

                lax.fori_loop(k + 1, steps, panel, 0)
                lax.fori_loop(k + 1, steps, row, 0)
                return carry

            lax.fori_loop(0, steps, eliminate, 0)

        corner = width // 2
        first = nn(turned[0:corner, :], solved_e[:, 0:corner])
        second = nn(turned[corner:width, :], solved_e[:, corner:width])
        folded, diagonal = fold(first, second, places(corner))
        folded_out[0:corner, :] = folded.astype(BF16)
        folded_out[corner:, :] = jnp.broadcast_to(diagonal, (PAD, corner)).astype(BF16)
        corner_out[...] = nn(turned[0:corner, :], solved_e[:, corner:width]).astype(BF16)


def fold(first, second, strict):
    rows, columns = strict
    return jnp.where(rows <= columns, first, second), diagonal_row(second, rows == columns)


def unfold(folded, diagonal, strict):
    rows, columns = strict
    turned = folded.T
    first = jnp.where(rows <= columns, folded, turned)
    second = jnp.where(rows > columns, folded, jnp.where(rows < columns, turned, diagonal))
    return first, second


ANY = pl.BlockSpec(memory_space=pl.ANY)
VMEM = pl.BlockSpec(memory_space=pltpu.VMEM)
SMEM = pl.BlockSpec(memory_space=pltpu.SMEM)


def cost(flops, bytes_accessed):
    return pl.CostEstimate(flops=flops, bytes_accessed=bytes_accessed, transcendentals=0)


def params(mib):
    return pltpu.CompilerParams(vmem_limit_bytes=mib * 2**20)


def eliminate(flags, own_d, other_d, e, r):
    size, block = own_d.shape[0], BLOCK
    width = e.shape[1]
    return pl.pallas_call(
        eliminate_kernel,
        out_shape=(
            jax.ShapeDtypeStruct(e.shape, BF16),
            jax.ShapeDtypeStruct(r.shape, BF16),
            jax.ShapeDtypeStruct((width // 2, width // 2), BF16),
            jax.ShapeDtypeStruct((width // 2 + PAD, width // 2), BF16),
        ),
        in_specs=[SMEM, ANY, VMEM, ANY, ANY],
        out_specs=(VMEM, VMEM, VMEM, VMEM),
        scratch_shapes=[
            pltpu.VMEM((size, size), BF16),
            pltpu.VMEM((size, size), F32),
            pltpu.VMEM(e.shape, BF16),
            pltpu.VMEM(r.shape, BF16),
            pltpu.VMEM(r.shape, F32),
            pltpu.VMEM((block, size), BF16),
            pltpu.VMEM((block, size), BF16),
            pltpu.VMEM((size, size), BF16),
            pltpu.VMEM((size, size), BF16),
            pltpu.VMEM(e.shape, BF16),
            pltpu.VMEM((width, size), BF16),
            pltpu.VMEM((-(-(size // block) // 8) * 8, block), F32),
            pltpu.VMEM((block, block), F32),
            pltpu.VMEM((block, block), F32),
            pltpu.SemaphoreType.DMA((3, size // block)),
        ],
        compiler_params=params(46),
        cost_estimate=cost(28 * 10**9, 16 * 2**20),
    )(flags, own_d, other_d, e, r)


def tip_kernel(flags, own_r, other_r, out):
    width = own_r.shape[0]

    @pl.when(flags[0] == 0)
    def _():
        out[...] = jnp.zeros_like(out)

    @pl.when(jnp.logical_and(flags[0] != 0, flags[1] == 0))
    def _():
        out[0:width, :] = nt(own_r[...], other_r[...]).astype(BF16)
        out[width:, :] = jnp.zeros((out.shape[0] - width, width), BF16)

    @pl.when(jnp.logical_and(flags[0] != 0, flags[1] != 0))
    def _():
        first = nt(other_r[...], other_r[...])
        second = nt(own_r[...], own_r[...])
        folded, diagonal = fold(first, second, places(width))
        out[0:width, :] = folded.astype(BF16)
        out[width:, :] = jnp.broadcast_to(diagonal, (out.shape[0] - width, width)).astype(BF16)


def tip_term(flags, own_r, other_r):
    width = own_r.shape[0]
    return pl.pallas_call(
        tip_kernel,
        out_shape=jax.ShapeDtypeStruct((width + 64, width), BF16),
        in_specs=[SMEM, VMEM, VMEM],
        out_specs=VMEM,
        compiler_params=params(16),
        cost_estimate=cost(10**9, 3 * 2**20),
    )(flags, own_r, other_r)


def arrow_kernel(flags, own_r, other_r, own_e, *outs):
    rows = own_r.shape[0]
    share = 2 * rows // len(outs)
    active, core = flags[2], flags[1]

    @pl.when(active == 0)
    def _():
        for out in outs:
            out[...] = jnp.zeros_like(out)

    def write(first, second):
        for source, base in ((first, 0), (second, rows)):
            value = (-nn(source[...], own_e[...])).astype(BF16)
            for i, out in enumerate(outs):
                low, high = max(base, i * share), min(base + rows, (i + 1) * share)
                if low < high:
                    out[low - i * share:high - i * share, :] = value[low - base:high - base, :]

    @pl.when(jnp.logical_and(active != 0, core == 0))
    def _():
        write(own_r, other_r)

    @pl.when(jnp.logical_and(active != 0, core != 0))
    def _():
        write(other_r, own_r)


def arrow_terms(flags, own_r, other_r, own_e):
    piece = jax.ShapeDtypeStruct((2 * own_r.shape[0] // PIECES, own_e.shape[1]), BF16)
    return pl.pallas_call(
        arrow_kernel,
        out_shape=(piece,) * PIECES,
        in_specs=[SMEM, VMEM, VMEM, VMEM],
        out_specs=(VMEM,) * PIECES,
        compiler_params=params(24),
        cost_estimate=cost(2 * 10**9, 6 * 2**20),
    )(flags, own_r, other_r, own_e)


def cross_kernel(flags, own_e, other_e, out):
    width = own_e.shape[1]
    half = width // 2

    @pl.when(flags[2] == 0)
    def _():
        out[...] = jnp.zeros_like(out)

    @pl.when(jnp.logical_and(flags[2] != 0, flags[1] == 0))
    def _():
        out[...] = nn(other_e[:, 0:half].T, own_e[...]).astype(BF16)

    @pl.when(jnp.logical_and(flags[2] != 0, flags[1] != 0))
    def _():
        out[...] = nn(own_e[:, half:width].T, other_e[...]).astype(BF16)


def cross_term(flags, own_e, other_e):
    width = own_e.shape[1]
    return pl.pallas_call(
        cross_kernel,
        out_shape=jax.ShapeDtypeStruct((width // 2, width), BF16),
        in_specs=[SMEM, VMEM, VMEM],
        out_specs=VMEM,
        compiler_params=params(24),
        cost_estimate=cost(2 * 10**9, 6 * 2**20),
    )(flags, own_e, other_e)


def separator_kernel(flags, separator, corner_in, folded, own_cross, other_cross, out):
    width = separator.shape[1]
    half = width // 2
    core = flags[1]
    first, second = unfold(
        folded[0:half, :].astype(F32), folded[half:half + 1, :].astype(F32), places(half)
    )
    corner = corner_in[...].astype(F32)
    base = pl.multiple_of(core * width, width)

    def less(rows, columns, term):
        out[rows, columns] = (separator[rows, columns].astype(F32) - term).astype(BF16)

    top, bottom = pl.ds(base, half), pl.ds(base + half, half)
    left, right = slice(0, half), slice(half, width)
    less(top, left, first)
    less(top, right, corner)
    less(bottom, left, corner.T)
    less(bottom, right, second)

    @pl.when(core == 0)
    def _():
        less(slice(width, width + half), slice(0, width), own_cross[...].astype(F32))
        less(slice(width + half, 2 * width), slice(0, width), other_cross[...].astype(F32))

    @pl.when(core != 0)
    def _():
        less(slice(0, width), left, other_cross[...].astype(F32).T)
        less(slice(0, width), right, own_cross[...].astype(F32).T)


def separator_less(flags, separator, corner, folded, own_cross, other_cross):
    return pl.pallas_call(
        separator_kernel,
        out_shape=jax.ShapeDtypeStruct(separator.shape, BF16),
        in_specs=[SMEM] + [VMEM] * 5,
        out_specs=VMEM,
        compiler_params=params(24),
        cost_estimate=cost(10**6, 6 * 2**20),
    )(flags, separator, corner, folded, own_cross, other_cross)


def new_tip_kernel(flags, tip, own_sum, other_sum, out):
    width = tip.shape[1]
    core = flags[1]

    @pl.when(core == 0)
    def _():
        first, _ = unfold(
            other_sum[0:width, :].astype(F32), other_sum[width:width + 1, :].astype(F32), places(width)
        )
        out[0:width, :] = tip[0:width, :].astype(F32) - first
        out[width:, :] = tip[width:, :].astype(F32) - own_sum[0:width, :].astype(F32).T

    @pl.when(core != 0)
    def _():
        _, second = unfold(
            own_sum[0:width, :].astype(F32), own_sum[width:width + 1, :].astype(F32), places(width)
        )
        out[0:width, :] = tip[0:width, :].astype(F32) - other_sum[0:width, :].astype(F32)
        out[width:, :] = tip[width:, :].astype(F32) - second


def tip_less(flags, tip, own_sum, other_sum):
    return pl.pallas_call(
        new_tip_kernel,
        out_shape=jax.ShapeDtypeStruct(tip.shape, F32),
        in_specs=[SMEM, VMEM, VMEM, VMEM],
        out_specs=VMEM,
        compiler_params=params(16),
        cost_estimate=cost(10**6, 3 * 2**20),
    )(flags, tip, own_sum, other_sum)


def swapped(x):
    return lax.ppermute(x, "space", [(0, 1), (1, 0)])


def to_previous(x):
    count = lax.axis_size("tm")
    return lax.ppermute(x, "tm", [(i, i - 1) for i in range(1, count)])


def added(*terms):
    return sum(term.astype(F32) for term in terms).astype(BF16)


def among_odd(x, distance, cyclic):
    count = lax.axis_size("tm") // 2
    if cyclic:
        group = min(SHARDS, count)
        pairs = [(i, i // group * group + (i + distance) % group) for i in range(count)]
    else:
        pairs = [(i, i ^ distance) for i in range(count)]
    return lax.ppermute(x, "tm", [(2 * i + 1, 2 * j + 1) for i, j in pairs])


def summed(term):
    count = lax.axis_size("tm")
    term = added(term, lax.ppermute(term, "tm", [(i, i + 1) for i in range(0, count, 2)]))
    odd_count = count // 2
    group = min(SHARDS, odd_count)
    place = (lax.axis_index("tm") // 2) % group
    share = term.shape[0] // group
    stacked = term.reshape(group, share, term.shape[1])

    def shard(i):
        return lax.dynamic_index_in_dim(stacked, i % group, 0, keepdims=False)

    parts = [among_odd(shard(place + d), d, True) for d in range(1, group)]
    own = added(shard(place), *parts)
    distance = group
    while distance < odd_count:
        own = added(own, among_odd(own, distance, False))
        distance *= 2
    whole = jnp.zeros_like(stacked)
    whole = lax.dynamic_update_index_in_dim(whole, own, place, 0)
    for d in range(1, group):
        part = among_odd(own, d, True)
        whole = lax.dynamic_update_index_in_dim(whole, part, (place - d) % group, 0)
    whole = whole.reshape(term.shape)
    returned = lax.ppermute(whole, "tm", [(i + 1, i) for i in range(0, count, 2)])
    return jnp.where(lax.axis_index("tm") % 2 == 0, returned, whole)


def on_device(interior_diag, coupling, arrow_rows, separator_diag, tip, lengths):
    position = lax.axis_index("tm")
    active = lengths[position] == 2
    flags = jnp.stack(
        [active, lax.axis_index("space") != 0, jnp.logical_and(active, position != 0)]
    ).astype(jnp.int32)
    other_diag = swapped(interior_diag)
    own_e, own_r, corner, folded = eliminate(flags, interior_diag, other_diag, coupling, arrow_rows)
    corner = to_previous(corner)
    other_r = swapped(own_r)
    term = tip_term(flags, own_r, other_r)
    tip_sum = summed(term)
    folded = to_previous(folded)
    other_e = swapped(own_e)
    cross = cross_term(flags, own_e, other_e)
    cross = to_previous(cross)
    pieces = arrow_terms(flags, own_r, other_r, own_e)
    received = []
    for piece in pieces:
        received.append(to_previous(piece))
    other_cross = swapped(cross)
    new_separator = separator_less(flags, separator_diag, corner, folded, cross, other_cross)
    other_sum = swapped(tip_sum)
    new_tip = tip_less(flags, tip, tip_sum, other_sum)
    return (new_separator, jnp.concatenate(received, axis=0), new_tip)


def solution(mesh):
    return jax.shard_map(
        on_device,
        mesh=mesh,
        in_specs=(
            P(("groups", "tm"), "space"),
            P(("groups", "tm"), "space"),
            P(("groups", "tm", "space"), None),
            P(("groups", "tm"), "space"),
            P("groups", "space"),
            P("groups"),
        ),
        out_specs=(
            P(("groups", "tm"), "space"),
            P(("groups", "tm"), "space"),
            P("groups", "space"),
        ),
        check_vma=False,
    )
```

```python
import functools

import jax
import jax.numpy as jnp
from jax import lax
from jax.experimental import pallas as pl
from jax.experimental.pallas import tpu as pltpu
from jax.sharding import PartitionSpec as P


F32 = jnp.float32
BF16 = jnp.bfloat16
BLOCK = 256
NEAR = 0.03
MOST_STEPS = 60
STAGES = 7
PAD = 16


def split(x):
    high = x.astype(BF16)
    return high, (x - high.astype(F32)).astype(BF16)


def nn(a, b):
    return lax.dot_general(a, b, (((1,), (0,)), ((), ())), preferred_element_type=F32)


def nt(a, b):
    return lax.dot_general(a, b, (((1,), (1,)), ((), ())), preferred_element_type=F32)


def three(dot, a, b):
    return dot(a[0], b[0]) + (dot(a[0], b[1]) + dot(a[1], b[0]))


def total(x):
    return jnp.sum(x, keepdims=True)


def places(size):
    rows = lax.broadcasted_iota(jnp.int32, (size, size), 0)
    columns = lax.broadcasted_iota(jnp.int32, (size, size), 1)
    return rows, columns


def diagonal_row(x, on_diagonal):
    return jnp.sum(jnp.where(on_diagonal, x, 0.0), axis=0, keepdims=True)


def unit_scaled(a, on_diagonal):
    diagonal = jnp.where(on_diagonal, a, 0.0)
    scale_row = lax.rsqrt(jnp.sum(diagonal, axis=0, keepdims=True))
    scale_column = lax.rsqrt(jnp.sum(diagonal, axis=1, keepdims=True))
    return a * scale_row * scale_column, scale_row


def first_root(off, off_square, identity):
    bound = jnp.sqrt(jnp.sqrt(total(off_square * off_square)))
    c = jnp.minimum(1.0, 1.9 / (1.0 + bound))
    gap = c * off - (1.0 - c) * identity
    gap_square = c * c * off_square - (2 * c * (1 - c)) * off + ((1 - c) * (1 - c)) * identity
    return (jnp.sqrt(c) * (identity - 0.5 * gap + 0.375 * gap_square)).astype(BF16)


def root_stages(a, on_diagonal, identity, result):
    unit, scale_row = unit_scaled(a, on_diagonal)
    off = unit - identity
    off_high = off.astype(BF16)
    high, low = split(unit)
    yield
    off_square = nn(off_high, off_high)
    yield
    first = first_root(off, off_square, identity)
    yield
    product = split(nt(high, first) + nt(low, first))
    yield
    gap = nn(first, product[0]) + nn(first, product[1]) - identity
    gap_high = gap.astype(BF16)
    yield
    gap_square = nn(gap_high, gap_high)
    change = split(0.375 * gap_square - 0.5 * gap)
    yield
    root = first.astype(F32) + (nn(change[0], first) + nn(change[1], first))
    result.append(split(root * scale_row))
    result.append(gap_square)


def root_until_near(a, on_diagonal, identity, unit_ref, root_ref):
    unit, scale_row = unit_scaled(a, on_diagonal)
    off = unit - identity
    off_square = nn(off.astype(BF16), off.astype(BF16))
    unit_ref[...] = unit
    root_ref[...] = first_root(off, off_square, identity).astype(F32)

    def far(state):
        return jnp.logical_and(jnp.logical_not(state[0] <= NEAR**4), state[1] < MOST_STEPS)

    def step(state):
        root = split(root_ref[...])
        product = split(three(nt, split(unit_ref[...]), root))
        gap = three(nn, root, product) - identity
        gap_square = nn(gap.astype(BF16), gap.astype(BF16))
        change = split(0.375 * gap_square - 0.5 * gap)
        root_ref[...] += three(nn, change, root)
        return jnp.sum(gap_square * gap_square), state[1] + 1

    lax.while_loop(far, step, (jnp.float32(1.0), jnp.int32(0)))
    return split(root_ref[...] * scale_row)


def interleave(stages, fillers):
    share = -(-len(fillers) // STAGES)
    for _ in stages:
        for filler in fillers[:share]:
            filler()
        fillers = fillers[share:]
    for filler in fillers:
        filler()


def eliminate_kernel(
    flags, own_d, other_d, e_hbm, r_hbm, solved_e, solved_r, corner_out, folded_out,
    given, diag, e_in, r_in, left_r, high, low, factor_high, factor_low, rest_e, turned,
    near, unit_ref, root_ref, sems,
):
    size, block = diag.shape[0], unit_ref.shape[0]
    half, width = own_d.shape[1], e_in.shape[1]
    steps = size // block
    core = flags[1]

    def at(i):
        return slice(i * block, (i + 1) * block)

    def arrival(i, which):
        source = own_d if which == 0 else other_d
        side = core if which == 0 else 1 - core
        columns = pl.ds(pl.multiple_of(side * half, half), half)
        return pltpu.make_async_copy(source.at[at(i), :], given.at[at(i), columns], sems.at[which, i])

    rows, columns = places(block)
    on_diagonal = rows == columns
    identity = jnp.where(on_diagonal, 1.0, 0.0).astype(F32)
    e_copy = pltpu.make_async_copy(e_hbm, e_in, sems.at[2, 0])
    r_copy = pltpu.make_async_copy(r_hbm, r_in, sems.at[2, 1])

    def solve_e(k, root):
        part = e_in[at(k), :]
        if k == 0:
            value = nn(root[0], part) + nn(root[1], part)
        else:
            before = slice(0, k * block)
            left = (factor_high[at(k), before], factor_low[at(k), before])
            part = part.astype(F32) - three(nn, left, (solved_e[before, :], rest_e[before, :]))
            value = three(nn, root, split(part))
        solved_e[at(k), :], rest_e[at(k), :] = split(value)
        turned[:, at(k)] = value.T.astype(BF16)

    @pl.when(flags[0] == 0)
    def _():
        solved_e[...] = jnp.zeros_like(solved_e)
        solved_r[...] = jnp.zeros_like(solved_r)
        corner_out[...] = jnp.zeros_like(corner_out)
        folded_out[...] = jnp.zeros_like(folded_out)

    @pl.when(flags[0] != 0)
    def _():
        for i in range(steps):
            arrival(i, 0).start()
            arrival(i, 1).start()
        r_copy.start()
        e_copy.start()

        def take(i):
            arrival(i, 0).wait()
            arrival(i, 1).wait()
            diag[at(i), i * block:] = given[at(i), i * block:].astype(F32)

        def take_r():
            r_copy.wait()
            left_r[...] = r_in[...].astype(F32)

        take(0)
        result = []
        fillers = [functools.partial(take, i) for i in range(1, steps)] + [take_r, e_copy.wait]
        interleave(root_stages(diag[at(0), at(0)], on_diagonal, identity, result), fillers)
        for k in range(steps):
            root, gap_square = result
            near[k:k + 1, :] = jnp.sum(gap_square * gap_square, axis=0, keepdims=True)
            result, part_r = [], []

            def panel(j):
                value = three(nn, root, split(diag[at(k), at(j)]))
                high[:, at(j)], low[:, at(j)] = split(value)
                factor_high[at(j), at(k)], factor_low[at(j), at(k)] = split(value.T)

            def update(i, j):
                left = (factor_high[at(i), at(k)], factor_low[at(i), at(k)])
                diag[at(i), at(j)] -= three(nn, left, (high[:, at(j)], low[:, at(j)]))

            def solve_r():
                part_r.extend(split(three(nt, split(left_r[:, at(k)]), root)))
                solved_r[:, at(k)] = part_r[0]

            def update_r(i):
                left_r[:, at(i)] -= three(nn, part_r, (high[:, at(i)], low[:, at(i)]))

            fillers = [functools.partial(panel, j) for j in range(k + 2, steps)]
            fillers += [
                functools.partial(update, i, j)
                for i in range(k + 1, steps) for j in range(max(i, k + 2), steps)
            ]
            fillers.append(solve_r)
            fillers += [functools.partial(update_r, i) for i in range(k + 1, steps)]
            fillers.append(functools.partial(solve_e, k, root))
            if k + 1 < steps:
                panel(k + 1)
                update(k + 1, k + 1)
                stages = root_stages(diag[at(k + 1), at(k + 1)], on_diagonal, identity, result)
                interleave(stages, fillers)
            else:
                interleave((), fillers)
        worst = jnp.max(jnp.sum(near[0:steps, :], axis=1, keepdims=True))

        @pl.when(jnp.logical_not(worst <= NEAR**4))
        def _():
            for i in range(steps):
                diag[at(i), i * block:] = given[at(i), i * block:].astype(F32)
            left_r[...] = r_in[...].astype(F32)

            def spot(i):
                return pl.ds(pl.multiple_of(i * block, block), block)

            def eliminate(k, carry):
                now = spot(k)
                root = root_until_near(diag[now, now], on_diagonal, identity, unit_ref, root_ref)
                part_r = split(three(nt, split(left_r[:, now]), root))
                solved_r[:, now] = part_r[0]

                def left_of(j, part):
                    there = spot(j)
                    left = (factor_high[now, there], factor_low[now, there])
                    return part - three(nn, left, (solved_e[there, :], rest_e[there, :]))

                part_e = lax.fori_loop(0, k, left_of, e_in[now, :].astype(F32))
                value = three(nn, root, split(part_e))
                solved_e[now, :], rest_e[now, :] = split(value)
                turned[:, now] = value.T.astype(BF16)

                def panel(j, carry):
                    there = spot(j)
                    value = three(nn, root, split(diag[now, there]))
                    high[:, there], low[:, there] = split(value)
                    factor_high[there, now], factor_low[there, now] = split(value.T)
                    left_r[:, there] -= three(nn, part_r, (high[:, there], low[:, there]))
                    return carry

                def row(i, carry):
                    here = spot(i)
                    left = (factor_high[here, now], factor_low[here, now])

                    def update(j, carry):
                        there = spot(j)
                        diag[here, there] -= three(nn, left, (high[:, there], low[:, there]))
                        return carry

                    return lax.fori_loop(i, steps, update, carry)

                lax.fori_loop(k + 1, steps, panel, 0)
                lax.fori_loop(k + 1, steps, row, 0)
                return carry

            lax.fori_loop(0, steps, eliminate, 0)

        corner = width // 2
        first = nn(turned[0:corner, :], solved_e[:, 0:corner])
        second = nn(turned[corner:width, :], solved_e[:, corner:width])
        folded, diagonal = fold(first, second, places(corner))
        folded_out[0:corner, :] = folded.astype(BF16)
        folded_out[corner:, :] = jnp.broadcast_to(diagonal, (PAD, corner)).astype(BF16)
        corner_out[...] = nn(turned[0:corner, :], solved_e[:, corner:width]).astype(BF16)


def fold(first, second, strict):
    rows, columns = strict
    return jnp.where(rows <= columns, first, second), diagonal_row(second, rows == columns)


def unfold(folded, diagonal, strict):
    rows, columns = strict
    turned = folded.T
    first = jnp.where(rows <= columns, folded, turned)
    second = jnp.where(rows > columns, folded, jnp.where(rows < columns, turned, diagonal))
    return first, second


ANY = pl.BlockSpec(memory_space=pl.ANY)
VMEM = pl.BlockSpec(memory_space=pltpu.VMEM)
SMEM = pl.BlockSpec(memory_space=pltpu.SMEM)


def cost(flops, bytes_accessed):
    return pl.CostEstimate(flops=flops, bytes_accessed=bytes_accessed, transcendentals=0)


def params(mib):
    return pltpu.CompilerParams(vmem_limit_bytes=mib * 2**20)


def eliminate(flags, own_d, other_d, e, r):
    size, block = own_d.shape[0], BLOCK
    width = e.shape[1]
    return pl.pallas_call(
        eliminate_kernel,
        out_shape=(
            jax.ShapeDtypeStruct(e.shape, BF16),
            jax.ShapeDtypeStruct(r.shape, BF16),
            jax.ShapeDtypeStruct((width // 2, width // 2), BF16),
            jax.ShapeDtypeStruct((width // 2 + PAD, width // 2), BF16),
        ),
        in_specs=[SMEM, ANY, VMEM, ANY, ANY],
        out_specs=(VMEM, VMEM, VMEM, VMEM),
        scratch_shapes=[
            pltpu.VMEM((size, size), BF16),
            pltpu.VMEM((size, size), F32),
            pltpu.VMEM(e.shape, BF16),
            pltpu.VMEM(r.shape, BF16),
            pltpu.VMEM(r.shape, F32),
            pltpu.VMEM((block, size), BF16),
            pltpu.VMEM((block, size), BF16),
            pltpu.VMEM((size, size), BF16),
            pltpu.VMEM((size, size), BF16),
            pltpu.VMEM(e.shape, BF16),
            pltpu.VMEM((width, size), BF16),
            pltpu.VMEM((-(-(size // block) // 8) * 8, block), F32),
            pltpu.VMEM((block, block), F32),
            pltpu.VMEM((block, block), F32),
            pltpu.SemaphoreType.DMA((3, size // block)),
        ],
        compiler_params=params(54),
        cost_estimate=cost(28 * 10**9, 16 * 2**20),
    )(flags, own_d, other_d, e, r)


def tip_kernel(flags, own_r, other_r, out):
    width = own_r.shape[0]

    @pl.when(flags[0] == 0)
    def _():
        out[...] = jnp.zeros_like(out)

    @pl.when(jnp.logical_and(flags[0] != 0, flags[1] == 0))
    def _():
        out[0:width, :] = nt(own_r[...], other_r[...]).astype(BF16)
        out[width:, :] = jnp.zeros((out.shape[0] - width, width), BF16)

    @pl.when(jnp.logical_and(flags[0] != 0, flags[1] != 0))
    def _():
        first = nt(other_r[...], other_r[...])
        second = nt(own_r[...], own_r[...])
        folded, diagonal = fold(first, second, places(width))
        out[0:width, :] = folded.astype(BF16)
        out[width:, :] = jnp.broadcast_to(diagonal, (out.shape[0] - width, width)).astype(BF16)


def tip_term(flags, own_r, other_r):
    width = own_r.shape[0]
    return pl.pallas_call(
        tip_kernel,
        out_shape=jax.ShapeDtypeStruct((width + 64, width), BF16),
        in_specs=[SMEM, VMEM, VMEM],
        out_specs=VMEM,
        compiler_params=params(16),
        cost_estimate=cost(10**9, 3 * 2**20),
    )(flags, own_r, other_r)


def arrow_kernel(flags, own_r, other_r, own_e, out):
    rows = own_r.shape[0]

    @pl.when(flags[2] == 0)
    def _():
        out[...] = jnp.zeros_like(out)

    @pl.when(flags[2] != 0)
    def _():
        core = flags[1]
        for source, side in ((own_r, core), (other_r, 1 - core)):
            place = pl.ds(pl.multiple_of(side * rows, rows), rows)
            out[place, :] = (-nn(source[...], own_e[...])).astype(BF16)


def arrow_term(flags, own_r, other_r, own_e):
    return pl.pallas_call(
        arrow_kernel,
        out_shape=jax.ShapeDtypeStruct((2 * own_r.shape[0], own_e.shape[1]), BF16),
        in_specs=[SMEM, VMEM, VMEM, VMEM],
        out_specs=VMEM,
        compiler_params=params(24),
        cost_estimate=cost(2 * 10**9, 6 * 2**20),
    )(flags, own_r, other_r, own_e)


def cross_kernel(flags, own_e, other_e, out):
    width = own_e.shape[1]
    half = width // 2

    @pl.when(flags[2] == 0)
    def _():
        out[...] = jnp.zeros_like(out)

    @pl.when(jnp.logical_and(flags[2] != 0, flags[1] == 0))
    def _():
        out[...] = nn(other_e[:, 0:half].T, own_e[...]).astype(BF16)

    @pl.when(jnp.logical_and(flags[2] != 0, flags[1] != 0))
    def _():
        out[...] = nn(own_e[:, half:width].T, other_e[...]).astype(BF16)


def cross_term(flags, own_e, other_e):
    width = own_e.shape[1]
    return pl.pallas_call(
        cross_kernel,
        out_shape=jax.ShapeDtypeStruct((width // 2, width), BF16),
        in_specs=[SMEM, VMEM, VMEM],
        out_specs=VMEM,
        compiler_params=params(24),
        cost_estimate=cost(2 * 10**9, 6 * 2**20),
    )(flags, own_e, other_e)


def separator_kernel(flags, separator, corner_in, folded, own_cross, other_cross, out):
    width = separator.shape[1]
    half = width // 2
    core = flags[1]
    first, second = unfold(
        folded[0:half, :].astype(F32), folded[half:half + 1, :].astype(F32), places(half)
    )
    corner = corner_in[...].astype(F32)
    base = pl.multiple_of(core * width, width)

    def less(rows, columns, term):
        out[rows, columns] = (separator[rows, columns].astype(F32) - term).astype(BF16)

    top, bottom = pl.ds(base, half), pl.ds(base + half, half)
    left, right = slice(0, half), slice(half, width)
    less(top, left, first)
    less(top, right, corner)
    less(bottom, left, corner.T)
    less(bottom, right, second)

    @pl.when(core == 0)
    def _():
        less(slice(width, width + half), slice(0, width), own_cross[...].astype(F32))
        less(slice(width + half, 2 * width), slice(0, width), other_cross[...].astype(F32))

    @pl.when(core != 0)
    def _():
        less(slice(0, width), left, other_cross[...].astype(F32).T)
        less(slice(0, width), right, own_cross[...].astype(F32).T)


def separator_less(flags, separator, corner, folded, own_cross, other_cross):
    return pl.pallas_call(
        separator_kernel,
        out_shape=jax.ShapeDtypeStruct(separator.shape, BF16),
        in_specs=[SMEM] + [VMEM] * 5,
        out_specs=VMEM,
        compiler_params=params(24),
        cost_estimate=cost(10**6, 6 * 2**20),
    )(flags, separator, corner, folded, own_cross, other_cross)


def new_tip_kernel(flags, tip, own_sum, other_sum, out):
    width = tip.shape[1]
    core = flags[1]

    @pl.when(core == 0)
    def _():
        first, _ = unfold(
            other_sum[0:width, :].astype(F32), other_sum[width:width + 1, :].astype(F32), places(width)
        )
        out[0:width, :] = tip[0:width, :].astype(F32) - first
        out[width:, :] = tip[width:, :].astype(F32) - own_sum[0:width, :].astype(F32).T

    @pl.when(core != 0)
    def _():
        _, second = unfold(
            own_sum[0:width, :].astype(F32), own_sum[width:width + 1, :].astype(F32), places(width)
        )
        out[0:width, :] = tip[0:width, :].astype(F32) - other_sum[0:width, :].astype(F32)
        out[width:, :] = tip[width:, :].astype(F32) - second


def tip_less(flags, tip, own_sum, other_sum):
    return pl.pallas_call(
        new_tip_kernel,
        out_shape=jax.ShapeDtypeStruct(tip.shape, F32),
        in_specs=[SMEM, VMEM, VMEM, VMEM],
        out_specs=VMEM,
        compiler_params=params(16),
        cost_estimate=cost(10**6, 3 * 2**20),
    )(flags, tip, own_sum, other_sum)


def swapped(x):
    return lax.ppermute(x, "space", [(0, 1), (1, 0)])


def to_previous(x):
    count = lax.axis_size("tm")
    return lax.ppermute(x, "tm", [(i, i - 1) for i in range(1, count)])


def on_device(interior_diag, coupling, arrow_rows, separator_diag, tip, lengths):
    position = lax.axis_index("tm")
    active = lengths[position] == 2
    flags = jnp.stack(
        [active, lax.axis_index("space") != 0, jnp.logical_and(active, position != 0)]
    ).astype(jnp.int32)
    other_diag = swapped(interior_diag)
    own_e, own_r, corner, folded = eliminate(flags, interior_diag, other_diag, coupling, arrow_rows)
    corner = to_previous(corner)
    folded = to_previous(folded)
    other_e = swapped(own_e)
    other_r = swapped(own_r)
    cross = cross_term(flags, own_e, other_e)
    cross = to_previous(cross)
    arrow = arrow_term(flags, own_r, other_r, own_e)
    arrow_fill = to_previous(arrow)
    term = tip_term(flags, own_r, other_r)
    tip_sum = lax.psum(term, "tm")
    other_cross = swapped(cross)
    new_separator = separator_less(flags, separator_diag, corner, folded, cross, other_cross)
    other_sum = swapped(tip_sum)
    new_tip = tip_less(flags, tip, tip_sum, other_sum)
    return (new_separator, arrow_fill, new_tip)


def solution(mesh):
    return jax.shard_map(
        on_device,
        mesh=mesh,
        in_specs=(
            P(("groups", "tm"), "space"),
            P(("groups", "tm"), "space"),
            P(("groups", "tm", "space"), None),
            P(("groups", "tm"), "space"),
            P("groups", "space"),
            P("groups"),
        ),
        out_specs=(
            P(("groups", "tm"), "space"),
            P(("groups", "tm"), "space"),
            P("groups", "space"),
        ),
        check_vma=False,
    )
```

```python
import functools

import jax
import jax.numpy as jnp
from jax import lax
from jax.experimental import pallas as pl
from jax.experimental.pallas import tpu as pltpu
from jax.sharding import PartitionSpec as P


F32 = jnp.float32
BF16 = jnp.bfloat16
BLOCK = 256
NEAR = 0.03
MOST_STEPS = 60
STAGES = 7
PAD = 16
PIECES = 3


def split(x):
    high = x.astype(BF16)
    return high, (x - high.astype(F32)).astype(BF16)


def nn(a, b):
    return lax.dot_general(a, b, (((1,), (0,)), ((), ())), preferred_element_type=F32)


def nt(a, b):
    return lax.dot_general(a, b, (((1,), (1,)), ((), ())), preferred_element_type=F32)


def three(dot, a, b):
    return dot(a[0], b[0]) + (dot(a[0], b[1]) + dot(a[1], b[0]))


def total(x):
    return jnp.sum(x, keepdims=True)


def places(size):
    rows = lax.broadcasted_iota(jnp.int32, (size, size), 0)
    columns = lax.broadcasted_iota(jnp.int32, (size, size), 1)
    return rows, columns


def diagonal_row(x, on_diagonal):
    return jnp.sum(jnp.where(on_diagonal, x, 0.0), axis=0, keepdims=True)


def unit_scaled(a, on_diagonal):
    diagonal = jnp.where(on_diagonal, a, 0.0)
    scale_row = lax.rsqrt(jnp.sum(diagonal, axis=0, keepdims=True))
    scale_column = lax.rsqrt(jnp.sum(diagonal, axis=1, keepdims=True))
    return a * scale_row * scale_column, scale_row


def first_root(off, off_square, identity):
    bound = jnp.sqrt(jnp.sqrt(total(off_square * off_square)))
    c = jnp.minimum(1.0, 1.9 / (1.0 + bound))
    gap = c * off - (1.0 - c) * identity
    gap_square = c * c * off_square - (2 * c * (1 - c)) * off + ((1 - c) * (1 - c)) * identity
    return (jnp.sqrt(c) * (identity - 0.5 * gap + 0.375 * gap_square)).astype(BF16)


def root_stages(a, on_diagonal, identity, result):
    unit, scale_row = unit_scaled(a, on_diagonal)
    off = unit - identity
    off_high = off.astype(BF16)
    high, low = split(unit)
    yield
    off_square = nn(off_high, off_high)
    yield
    first = first_root(off, off_square, identity)
    yield
    product = split(nt(high, first) + nt(low, first))
    yield
    gap = nn(first, product[0]) + nn(first, product[1]) - identity
    gap_high = gap.astype(BF16)
    yield
    gap_square = nn(gap_high, gap_high)
    change = split(0.375 * gap_square - 0.5 * gap)
    yield
    root = first.astype(F32) + (nn(change[0], first) + nn(change[1], first))
    result.append(split(root * scale_row))
    result.append(gap_square)


def root_until_near(a, on_diagonal, identity, unit_ref, root_ref):
    unit, scale_row = unit_scaled(a, on_diagonal)
    off = unit - identity
    off_square = nn(off.astype(BF16), off.astype(BF16))
    unit_ref[...] = unit
    root_ref[...] = first_root(off, off_square, identity).astype(F32)

    def far(state):
        return jnp.logical_and(jnp.logical_not(state[0] <= NEAR**4), state[1] < MOST_STEPS)

    def step(state):
        root = split(root_ref[...])
        product = split(three(nt, split(unit_ref[...]), root))
        gap = three(nn, root, product) - identity
        gap_square = nn(gap.astype(BF16), gap.astype(BF16))
        change = split(0.375 * gap_square - 0.5 * gap)
        root_ref[...] += three(nn, change, root)
        return jnp.sum(gap_square * gap_square), state[1] + 1

    lax.while_loop(far, step, (jnp.float32(1.0), jnp.int32(0)))
    return split(root_ref[...] * scale_row)


def interleave(stages, fillers):
    share = -(-len(fillers) // STAGES)
    for _ in stages:
        for filler in fillers[:share]:
            filler()
        fillers = fillers[share:]
    for filler in fillers:
        filler()


def eliminate_kernel(
    flags, own_d, other_d, e_hbm, r_hbm, solved_e, solved_r, corner_out, folded_out,
    given, diag, e_in, r_in, left_e, left_r, high, low, high_t, low_t, turned,
    near, unit_ref, root_ref, sems,
):
    size, block = diag.shape[0], unit_ref.shape[0]
    half, width = own_d.shape[1], e_in.shape[1]
    steps = size // block
    core = flags[1]

    def at(i):
        return slice(i * block, (i + 1) * block)

    def arrival(i, which):
        source = own_d if which == 0 else other_d
        side = core if which == 0 else 1 - core
        columns = pl.ds(pl.multiple_of(side * half, half), half)
        return pltpu.make_async_copy(source.at[at(i), :], given.at[at(i), columns], sems.at[which, i])

    rows, columns = places(block)
    on_diagonal = rows == columns
    identity = jnp.where(on_diagonal, 1.0, 0.0).astype(F32)
    e_copy = pltpu.make_async_copy(e_hbm, e_in, sems.at[2, 0])
    r_copy = pltpu.make_async_copy(r_hbm, r_in, sems.at[2, 1])

    @pl.when(flags[0] == 0)
    def _():
        solved_e[...] = jnp.zeros_like(solved_e)
        solved_r[...] = jnp.zeros_like(solved_r)
        corner_out[...] = jnp.zeros_like(corner_out)
        folded_out[...] = jnp.zeros_like(folded_out)

    @pl.when(flags[0] != 0)
    def _():
        for i in range(steps):
            arrival(i, 0).start()
            arrival(i, 1).start()
        r_copy.start()
        e_copy.start()

        def take(i):
            arrival(i, 0).wait()
            arrival(i, 1).wait()
            diag[at(i), i * block:] = given[at(i), i * block:].astype(F32)

        def take_r():
            r_copy.wait()
            left_r[...] = r_in[...].astype(F32)

        def take_e():
            e_copy.wait()
            left_e[...] = e_in[...].astype(F32)

        take(0)
        result = []
        fillers = [functools.partial(take, i) for i in range(1, steps)] + [take_r, take_e]
        interleave(root_stages(diag[at(0), at(0)], on_diagonal, identity, result), fillers)
        for k in range(steps):
            root, gap_square = result
            near[k:k + 1, :] = jnp.sum(gap_square * gap_square, axis=0, keepdims=True)
            result, part_e, part_r = [], [], []

            def panel(j):
                value = three(nn, root, split(diag[at(k), at(j)]))
                high[:, at(j)], low[:, at(j)] = split(value)
                high_t[at(j), :], low_t[at(j), :] = split(value.T)

            def update(i, j):
                left = (high_t[at(i), :], low_t[at(i), :])
                diag[at(i), at(j)] -= three(nn, left, (high[:, at(j)], low[:, at(j)]))

            def solve_r():
                part_r.extend(split(three(nt, split(left_r[:, at(k)]), root)))
                solved_r[:, at(k)] = part_r[0]

            def update_r(i):
                left_r[:, at(i)] -= three(nn, part_r, (high[:, at(i)], low[:, at(i)]))

            def solve_e():
                value = three(nn, root, split(left_e[at(k), :]))
                part_e.extend(split(value))
                solved_e[at(k), :] = part_e[0]
                turned[:, at(k)] = value.T.astype(BF16)

            def update_e(i):
                left_e[at(i), :] -= three(nn, (high_t[at(i), :], low_t[at(i), :]), part_e)

            fillers = [functools.partial(panel, j) for j in range(k + 2, steps)]
            fillers += [
                functools.partial(update, i, j)
                for i in range(k + 1, steps) for j in range(max(i, k + 2), steps)
            ]
            fillers.append(solve_e)
            fillers += [functools.partial(update_e, i) for i in range(k + 1, steps)]
            fillers.append(solve_r)
            fillers += [functools.partial(update_r, i) for i in range(k + 1, steps)]
            if k + 1 < steps:
                panel(k + 1)
                update(k + 1, k + 1)
                stages = root_stages(diag[at(k + 1), at(k + 1)], on_diagonal, identity, result)
                interleave(stages, fillers)
            else:
                interleave((), fillers)
        worst = jnp.max(jnp.sum(near[0:steps, :], axis=1, keepdims=True))

        @pl.when(jnp.logical_not(worst <= NEAR**4))
        def _():
            for i in range(steps):
                diag[at(i), i * block:] = given[at(i), i * block:].astype(F32)
            left_e[...] = e_in[...].astype(F32)
            left_r[...] = r_in[...].astype(F32)

            def spot(i):
                return pl.ds(pl.multiple_of(i * block, block), block)

            def eliminate(k, carry):
                now = spot(k)
                root = root_until_near(diag[now, now], on_diagonal, identity, unit_ref, root_ref)
                part_r = split(three(nt, split(left_r[:, now]), root))
                solved_r[:, now] = part_r[0]

                value = three(nn, root, split(left_e[now, :]))
                part_e = split(value)
                solved_e[now, :] = part_e[0]
                turned[:, now] = value.T.astype(BF16)

                def panel(j, carry):
                    there = spot(j)
                    value = three(nn, root, split(diag[now, there]))
                    high[:, there], low[:, there] = split(value)
                    high_t[there, :], low_t[there, :] = split(value.T)
                    left_r[:, there] -= three(nn, part_r, (high[:, there], low[:, there]))
                    left = (high_t[there, :], low_t[there, :])
                    left_e[there, :] -= three(nn, left, part_e)
                    return carry

                def row(i, carry):
                    here = spot(i)
                    left = (high_t[here, :], low_t[here, :])

                    def update(j, carry):
                        there = spot(j)
                        diag[here, there] -= three(nn, left, (high[:, there], low[:, there]))
                        return carry

                    return lax.fori_loop(i, steps, update, carry)

                lax.fori_loop(k + 1, steps, panel, 0)
                lax.fori_loop(k + 1, steps, row, 0)
                return carry

            lax.fori_loop(0, steps, eliminate, 0)

        corner = width // 2
        first = nn(turned[0:corner, :], solved_e[:, 0:corner])
        second = nn(turned[corner:width, :], solved_e[:, corner:width])
        folded, diagonal = fold(first, second, places(corner))
        folded_out[0:corner, :] = folded.astype(BF16)
        folded_out[corner:, :] = jnp.broadcast_to(diagonal, (PAD, corner)).astype(BF16)
        corner_out[...] = nn(turned[0:corner, :], solved_e[:, corner:width]).astype(BF16)


def fold(first, second, strict):
    rows, columns = strict
    return jnp.where(rows <= columns, first, second), diagonal_row(second, rows == columns)


def unfold(folded, diagonal, strict):
    rows, columns = strict
    turned = folded.T
    first = jnp.where(rows <= columns, folded, turned)
    second = jnp.where(rows > columns, folded, jnp.where(rows < columns, turned, diagonal))
    return first, second


ANY = pl.BlockSpec(memory_space=pl.ANY)
VMEM = pl.BlockSpec(memory_space=pltpu.VMEM)
SMEM = pl.BlockSpec(memory_space=pltpu.SMEM)


def cost(flops, bytes_accessed):
    return pl.CostEstimate(flops=flops, bytes_accessed=bytes_accessed, transcendentals=0)


def params(mib):
    return pltpu.CompilerParams(vmem_limit_bytes=mib * 2**20)


def eliminate(flags, own_d, other_d, e, r):
    size, block = own_d.shape[0], BLOCK
    width = e.shape[1]
    return pl.pallas_call(
        eliminate_kernel,
        out_shape=(
            jax.ShapeDtypeStruct(e.shape, BF16),
            jax.ShapeDtypeStruct(r.shape, BF16),
            jax.ShapeDtypeStruct((width // 2, width // 2), BF16),
            jax.ShapeDtypeStruct((width // 2 + PAD, width // 2), BF16),
        ),
        in_specs=[SMEM, ANY, VMEM, ANY, ANY],
        out_specs=(VMEM, VMEM, VMEM, VMEM),
        scratch_shapes=[
            pltpu.VMEM((size, size), BF16),
            pltpu.VMEM((size, size), F32),
            pltpu.VMEM(e.shape, BF16),
            pltpu.VMEM(r.shape, BF16),
            pltpu.VMEM(e.shape, F32),
            pltpu.VMEM(r.shape, F32),
            pltpu.VMEM((block, size), BF16),
            pltpu.VMEM((block, size), BF16),
            pltpu.VMEM((size, block), BF16),
            pltpu.VMEM((size, block), BF16),
            pltpu.VMEM((width, size), BF16),
            pltpu.VMEM((-(-(size // block) // 8) * 8, block), F32),
            pltpu.VMEM((block, block), F32),
            pltpu.VMEM((block, block), F32),
            pltpu.SemaphoreType.DMA((3, size // block)),
        ],
        compiler_params=params(52),
        cost_estimate=cost(28 * 10**9, 16 * 2**20),
    )(flags, own_d, other_d, e, r)


def tip_kernel(flags, own_r, other_r, out):
    width = own_r.shape[0]

    @pl.when(flags[0] == 0)
    def _():
        out[...] = jnp.zeros_like(out)

    @pl.when(jnp.logical_and(flags[0] != 0, flags[1] == 0))
    def _():
        out[0:width, :] = nt(own_r[...], other_r[...]).astype(BF16)
        out[width:, :] = jnp.zeros((out.shape[0] - width, width), BF16)

    @pl.when(jnp.logical_and(flags[0] != 0, flags[1] != 0))
    def _():
        first = nt(other_r[...], other_r[...])
        second = nt(own_r[...], own_r[...])
        folded, diagonal = fold(first, second, places(width))
        out[0:width, :] = folded.astype(BF16)
        out[width:, :] = jnp.broadcast_to(diagonal, (out.shape[0] - width, width)).astype(BF16)


def tip_term(flags, own_r, other_r):
    width = own_r.shape[0]
    return pl.pallas_call(
        tip_kernel,
        out_shape=jax.ShapeDtypeStruct((width + PAD, width), BF16),
        in_specs=[SMEM, VMEM, VMEM],
        out_specs=VMEM,
        compiler_params=params(16),
        cost_estimate=cost(10**9, 3 * 2**20),
    )(flags, own_r, other_r)


def arrow_kernel(flags, own_r, other_r, own_e, *outs):
    rows = own_r.shape[0]
    share = 2 * rows // len(outs)
    active, core = flags[2], flags[1]

    @pl.when(active == 0)
    def _():
        for out in outs:
            out[...] = jnp.zeros_like(out)

    def write(first, second):
        for source, base in ((first, 0), (second, rows)):
            value = (-nn(source[...], own_e[...])).astype(BF16)
            for i, out in enumerate(outs):
                low, high = max(base, i * share), min(base + rows, (i + 1) * share)
                if low < high:
                    out[low - i * share:high - i * share, :] = value[low - base:high - base, :]

    @pl.when(jnp.logical_and(active != 0, core == 0))
    def _():
        write(own_r, other_r)

    @pl.when(jnp.logical_and(active != 0, core != 0))
    def _():
        write(other_r, own_r)


def arrow_terms(flags, own_r, other_r, own_e):
    piece = jax.ShapeDtypeStruct((2 * own_r.shape[0] // PIECES, own_e.shape[1]), BF16)
    return pl.pallas_call(
        arrow_kernel,
        out_shape=(piece,) * PIECES,
        in_specs=[SMEM, VMEM, VMEM, VMEM],
        out_specs=(VMEM,) * PIECES,
        compiler_params=params(24),
        cost_estimate=cost(2 * 10**9, 6 * 2**20),
    )(flags, own_r, other_r, own_e)


def cross_kernel(flags, own_e, other_e, out):
    width = own_e.shape[1]
    half = width // 2

    @pl.when(flags[2] == 0)
    def _():
        out[...] = jnp.zeros_like(out)

    @pl.when(jnp.logical_and(flags[2] != 0, flags[1] == 0))
    def _():
        out[...] = nn(other_e[:, 0:half].T, own_e[...]).astype(BF16)

    @pl.when(jnp.logical_and(flags[2] != 0, flags[1] != 0))
    def _():
        out[...] = nn(own_e[:, half:width].T, other_e[...]).astype(BF16)


def cross_term(flags, own_e, other_e):
    width = own_e.shape[1]
    return pl.pallas_call(
        cross_kernel,
        out_shape=jax.ShapeDtypeStruct((width // 2, width), BF16),
        in_specs=[SMEM, VMEM, VMEM],
        out_specs=VMEM,
        compiler_params=params(24),
        cost_estimate=cost(2 * 10**9, 6 * 2**20),
    )(flags, own_e, other_e)


def separator_kernel(flags, separator, corner_in, folded, own_cross, other_cross, out):
    width = separator.shape[1]
    half = width // 2
    core = flags[1]
    first, second = unfold(
        folded[0:half, :].astype(F32), folded[half:half + 1, :].astype(F32), places(half)
    )
    corner = corner_in[...].astype(F32)
    base = pl.multiple_of(core * width, width)

    def less(rows, columns, term):
        out[rows, columns] = (separator[rows, columns].astype(F32) - term).astype(BF16)

    top, bottom = pl.ds(base, half), pl.ds(base + half, half)
    left, right = slice(0, half), slice(half, width)
    less(top, left, first)
    less(top, right, corner)
    less(bottom, left, corner.T)
    less(bottom, right, second)

    @pl.when(core == 0)
    def _():
        less(slice(width, width + half), slice(0, width), own_cross[...].astype(F32))
        less(slice(width + half, 2 * width), slice(0, width), other_cross[...].astype(F32))

    @pl.when(core != 0)
    def _():
        less(slice(0, width), left, other_cross[...].astype(F32).T)
        less(slice(0, width), right, own_cross[...].astype(F32).T)


def separator_less(flags, separator, corner, folded, own_cross, other_cross):
    return pl.pallas_call(
        separator_kernel,
        out_shape=jax.ShapeDtypeStruct(separator.shape, BF16),
        in_specs=[SMEM] + [VMEM] * 5,
        out_specs=VMEM,
        compiler_params=params(24),
        cost_estimate=cost(10**6, 6 * 2**20),
    )(flags, separator, corner, folded, own_cross, other_cross)


def new_tip_kernel(flags, tip, own_sum, other_sum, out):
    width = tip.shape[1]
    core = flags[1]

    @pl.when(core == 0)
    def _():
        first, _ = unfold(
            other_sum[0:width, :].astype(F32), other_sum[width:width + 1, :].astype(F32), places(width)
        )
        out[0:width, :] = tip[0:width, :].astype(F32) - first
        out[width:, :] = tip[width:, :].astype(F32) - own_sum[0:width, :].astype(F32).T

    @pl.when(core != 0)
    def _():
        _, second = unfold(
            own_sum[0:width, :].astype(F32), own_sum[width:width + 1, :].astype(F32), places(width)
        )
        out[0:width, :] = tip[0:width, :].astype(F32) - other_sum[0:width, :].astype(F32)
        out[width:, :] = tip[width:, :].astype(F32) - second


def tip_less(flags, tip, own_sum, other_sum):
    return pl.pallas_call(
        new_tip_kernel,
        out_shape=jax.ShapeDtypeStruct(tip.shape, F32),
        in_specs=[SMEM, VMEM, VMEM, VMEM],
        out_specs=VMEM,
        compiler_params=params(16),
        cost_estimate=cost(10**6, 3 * 2**20),
    )(flags, tip, own_sum, other_sum)


def swapped(x):
    return lax.ppermute(x, "space", [(0, 1), (1, 0)])


def to_previous(x):
    count = lax.axis_size("tm")
    return lax.ppermute(x, "tm", [(i, i - 1) for i in range(1, count)])


def added(*terms):
    return sum(term.astype(F32) for term in terms).astype(BF16)


def summed(term):
    count = lax.axis_size("tm")
    term = added(term, lax.ppermute(term, "tm", [(i, i + 1) for i in range(0, count, 2)]))
    distance = 2
    while distance < count:
        pairs = [(i, i ^ distance) for i in range(1, count, 2)]
        term = added(term, lax.ppermute(term, "tm", pairs))
        distance *= 2
    returned = lax.ppermute(term, "tm", [(i + 1, i) for i in range(0, count, 2)])
    return jnp.where(lax.axis_index("tm") % 2 == 0, returned, term)


def on_device(interior_diag, coupling, arrow_rows, separator_diag, tip, lengths):
    position = lax.axis_index("tm")
    active = lengths[position] == 2
    flags = jnp.stack(
        [active, lax.axis_index("space") != 0, jnp.logical_and(active, position != 0)]
    ).astype(jnp.int32)
    other_diag = swapped(interior_diag)
    own_e, own_r, corner, folded = eliminate(flags, interior_diag, other_diag, coupling, arrow_rows)
    corner = to_previous(corner)
    other_r = swapped(own_r)
    term = tip_term(flags, own_r, other_r)
    tip_sum = summed(term)
    folded = to_previous(folded)
    other_e = swapped(own_e)
    cross = cross_term(flags, own_e, other_e)
    cross = to_previous(cross)
    pieces = arrow_terms(flags, own_r, other_r, own_e)
    received = []
    for piece in pieces:
        received.append(to_previous(piece))
    other_cross = swapped(cross)
    new_separator = separator_less(flags, separator_diag, corner, folded, cross, other_cross)
    other_sum = swapped(tip_sum)
    new_tip = tip_less(flags, tip, tip_sum, other_sum)
    arrow_fill = jnp.concatenate(received, axis=0)
    return (new_separator, arrow_fill, new_tip)


def solution(mesh):
    return jax.shard_map(
        on_device,
        mesh=mesh,
        in_specs=(
            P(("groups", "tm"), "space"),
            P(("groups", "tm"), "space"),
            P(("groups", "tm", "space"), None),
            P(("groups", "tm"), "space"),
            P("groups", "space"),
            P("groups"),
        ),
        out_specs=(
            P(("groups", "tm"), "space"),
            P(("groups", "tm"), "space"),
            P("groups", "space"),
        ),
        check_vma=False,
    )
```

```python
import functools

import jax
import jax.numpy as jnp
from jax import lax
from jax.experimental import pallas as pl
from jax.experimental.pallas import tpu as pltpu
from jax.sharding import PartitionSpec as P


F32 = jnp.float32
BF16 = jnp.bfloat16
BLOCK = 256
NEAR = 0.03
MOST_STEPS = 60
STAGES = 7
PAD = 16
PIECES = 3


def split(x):
    high = x.astype(BF16)
    return high, (x - high.astype(F32)).astype(BF16)


def nn(a, b):
    return lax.dot_general(a, b, (((1,), (0,)), ((), ())), preferred_element_type=F32)


def nt(a, b):
    return lax.dot_general(a, b, (((1,), (1,)), ((), ())), preferred_element_type=F32)


def three(dot, a, b):
    return dot(a[0], b[0]) + (dot(a[0], b[1]) + dot(a[1], b[0]))


def total(x):
    return jnp.sum(x, keepdims=True)


def places(size):
    rows = lax.broadcasted_iota(jnp.int32, (size, size), 0)
    columns = lax.broadcasted_iota(jnp.int32, (size, size), 1)
    return rows, columns


def diagonal_row(x, on_diagonal):
    return jnp.sum(jnp.where(on_diagonal, x, 0.0), axis=0, keepdims=True)


def unit_scaled(a, on_diagonal):
    diagonal = jnp.where(on_diagonal, a, 0.0)
    scale_row = lax.rsqrt(jnp.sum(diagonal, axis=0, keepdims=True))
    scale_column = lax.rsqrt(jnp.sum(diagonal, axis=1, keepdims=True))
    return a * scale_row * scale_column, scale_row


def first_root(off, off_square, identity):
    bound = jnp.sqrt(jnp.sqrt(total(off_square * off_square)))
    c = jnp.minimum(1.0, 1.9 / (1.0 + bound))
    gap = c * off - (1.0 - c) * identity
    gap_square = c * c * off_square - (2 * c * (1 - c)) * off + ((1 - c) * (1 - c)) * identity
    return (jnp.sqrt(c) * (identity - 0.5 * gap + 0.375 * gap_square)).astype(BF16)


def root_stages(a, on_diagonal, identity, result):
    unit, scale_row = unit_scaled(a, on_diagonal)
    off = unit - identity
    off_high = off.astype(BF16)
    high, low = split(unit)
    yield
    off_square = nn(off_high, off_high)
    yield
    first = first_root(off, off_square, identity)
    yield
    product = split(nt(high, first) + nt(low, first))
    yield
    gap = nn(first, product[0]) + nn(first, product[1]) - identity
    gap_high = gap.astype(BF16)
    yield
    gap_square = nn(gap_high, gap_high)
    change = split(0.375 * gap_square - 0.5 * gap)
    yield
    root = first.astype(F32) + (nn(change[0], first) + nn(change[1], first))
    result.append(split(root * scale_row))
    result.append(gap_square)


def root_until_near(a, on_diagonal, identity, unit_ref, root_ref):
    unit, scale_row = unit_scaled(a, on_diagonal)
    off = unit - identity
    off_square = nn(off.astype(BF16), off.astype(BF16))
    unit_ref[...] = unit
    root_ref[...] = first_root(off, off_square, identity).astype(F32)

    def far(state):
        return jnp.logical_and(jnp.logical_not(state[0] <= NEAR**4), state[1] < MOST_STEPS)

    def step(state):
        root = split(root_ref[...])
        product = split(three(nt, split(unit_ref[...]), root))
        gap = three(nn, root, product) - identity
        gap_square = nn(gap.astype(BF16), gap.astype(BF16))
        change = split(0.375 * gap_square - 0.5 * gap)
        root_ref[...] += three(nn, change, root)
        return jnp.sum(gap_square * gap_square), state[1] + 1

    lax.while_loop(far, step, (jnp.float32(1.0), jnp.int32(0)))
    return split(root_ref[...] * scale_row)


def interleave(stages, fillers):
    share = -(-len(fillers) // STAGES)
    for _ in stages:
        for filler in fillers[:share]:
            filler()
        fillers = fillers[share:]
    for filler in fillers:
        filler()


def eliminate_kernel(
    flags, own_d, other_d, e_hbm, r_hbm, solved_e, solved_r, corner_out, folded_out,
    given, diag, e_in, r_in, left_e, left_r, high, low, high_t, low_t, turned,
    near, unit_ref, root_ref, sems,
):
    size, block = diag.shape[0], unit_ref.shape[0]
    half, width = own_d.shape[1], e_in.shape[1]
    steps = size // block
    core = flags[1]

    def at(i):
        return slice(i * block, (i + 1) * block)

    def arrival(i, which):
        source = own_d if which == 0 else other_d
        side = core if which == 0 else 1 - core
        columns = pl.ds(pl.multiple_of(side * half, half), half)
        return pltpu.make_async_copy(source.at[at(i), :], given.at[at(i), columns], sems.at[which, i])

    rows, columns = places(block)
    on_diagonal = rows == columns
    identity = jnp.where(on_diagonal, 1.0, 0.0).astype(F32)
    e_copy = pltpu.make_async_copy(e_hbm, e_in, sems.at[2, 0])
    r_copy = pltpu.make_async_copy(r_hbm, r_in, sems.at[2, 1])

    @pl.when(flags[0] == 0)
    def _():
        solved_e[...] = jnp.zeros_like(solved_e)
        solved_r[...] = jnp.zeros_like(solved_r)
        corner_out[...] = jnp.zeros_like(corner_out)
        folded_out[...] = jnp.zeros_like(folded_out)

    @pl.when(flags[0] != 0)
    def _():
        for i in range(steps):
            arrival(i, 0).start()
            arrival(i, 1).start()
        r_copy.start()
        e_copy.start()

        def take(i):
            arrival(i, 0).wait()
            arrival(i, 1).wait()
            diag[at(i), i * block:] = given[at(i), i * block:].astype(F32)

        def take_r():
            r_copy.wait()
            left_r[...] = r_in[...].astype(F32)

        def take_e():
            e_copy.wait()
            left_e[...] = e_in[...].astype(F32)

        take(0)
        result = []
        fillers = [functools.partial(take, i) for i in range(1, steps)] + [take_r, take_e]
        interleave(root_stages(diag[at(0), at(0)], on_diagonal, identity, result), fillers)
        for k in range(steps):
            root, gap_square = result
            near[k:k + 1, :] = jnp.sum(gap_square * gap_square, axis=0, keepdims=True)
            result, part_e, part_r = [], [], []

            def panel(j):
                value = three(nn, root, split(diag[at(k), at(j)]))
                high[:, at(j)], low[:, at(j)] = split(value)
                high_t[at(j), :], low_t[at(j), :] = split(value.T)

            def update(i, j):
                left = (high_t[at(i), :], low_t[at(i), :])
                diag[at(i), at(j)] -= three(nn, left, (high[:, at(j)], low[:, at(j)]))

            def solve_r():
                part_r.extend(split(three(nt, split(left_r[:, at(k)]), root)))
                solved_r[:, at(k)] = part_r[0]

            def update_r(i):
                left_r[:, at(i)] -= three(nn, part_r, (high[:, at(i)], low[:, at(i)]))

            def solve_e():
                value = three(nn, root, split(left_e[at(k), :]))
                part_e.extend(split(value))
                solved_e[at(k), :] = part_e[0]
                turned[:, at(k)] = value.T.astype(BF16)

            def update_e(i):
                left_e[at(i), :] -= three(nn, (high_t[at(i), :], low_t[at(i), :]), part_e)

            fillers = [functools.partial(panel, j) for j in range(k + 2, steps)]
            fillers += [
                functools.partial(update, i, j)
                for i in range(k + 1, steps) for j in range(max(i, k + 2), steps)
            ]
            fillers.append(solve_e)
            fillers += [functools.partial(update_e, i) for i in range(k + 1, steps)]
            fillers.append(solve_r)
            fillers += [functools.partial(update_r, i) for i in range(k + 1, steps)]
            if k + 1 < steps:
                panel(k + 1)
                update(k + 1, k + 1)
                stages = root_stages(diag[at(k + 1), at(k + 1)], on_diagonal, identity, result)
                interleave(stages, fillers)
            else:
                interleave((), fillers)
        worst = jnp.max(jnp.sum(near[0:steps, :], axis=1, keepdims=True))

        @pl.when(jnp.logical_not(worst <= NEAR**4))
        def _():
            for i in range(steps):
                diag[at(i), i * block:] = given[at(i), i * block:].astype(F32)
            left_e[...] = e_in[...].astype(F32)
            left_r[...] = r_in[...].astype(F32)

            def spot(i):
                return pl.ds(pl.multiple_of(i * block, block), block)

            def eliminate(k, carry):
                now = spot(k)
                root = root_until_near(diag[now, now], on_diagonal, identity, unit_ref, root_ref)
                part_r = split(three(nt, split(left_r[:, now]), root))
                solved_r[:, now] = part_r[0]

                value = three(nn, root, split(left_e[now, :]))
                part_e = split(value)
                solved_e[now, :] = part_e[0]
                turned[:, now] = value.T.astype(BF16)

                def panel(j, carry):
                    there = spot(j)
                    value = three(nn, root, split(diag[now, there]))
                    high[:, there], low[:, there] = split(value)
                    high_t[there, :], low_t[there, :] = split(value.T)
                    left_r[:, there] -= three(nn, part_r, (high[:, there], low[:, there]))
                    left = (high_t[there, :], low_t[there, :])
                    left_e[there, :] -= three(nn, left, part_e)
                    return carry

                def row(i, carry):
                    here = spot(i)
                    left = (high_t[here, :], low_t[here, :])

                    def update(j, carry):
                        there = spot(j)
                        diag[here, there] -= three(nn, left, (high[:, there], low[:, there]))
                        return carry

                    return lax.fori_loop(i, steps, update, carry)

                lax.fori_loop(k + 1, steps, panel, 0)
                lax.fori_loop(k + 1, steps, row, 0)
                return carry

            lax.fori_loop(0, steps, eliminate, 0)

        corner = width // 2
        first = nn(turned[0:corner, :], solved_e[:, 0:corner])
        second = nn(turned[corner:width, :], solved_e[:, corner:width])
        folded, diagonal = fold(first, second, places(corner))
        folded_out[0:corner, :] = folded.astype(BF16)
        folded_out[corner:, :] = jnp.broadcast_to(diagonal, (PAD, corner)).astype(BF16)
        corner_out[...] = nn(turned[0:corner, :], solved_e[:, corner:width]).astype(BF16)


def fold(first, second, strict):
    rows, columns = strict
    return jnp.where(rows <= columns, first, second), diagonal_row(second, rows == columns)


def unfold(folded, diagonal, strict):
    rows, columns = strict
    turned = folded.T
    first = jnp.where(rows <= columns, folded, turned)
    second = jnp.where(rows > columns, folded, jnp.where(rows < columns, turned, diagonal))
    return first, second


ANY = pl.BlockSpec(memory_space=pl.ANY)
VMEM = pl.BlockSpec(memory_space=pltpu.VMEM)
SMEM = pl.BlockSpec(memory_space=pltpu.SMEM)


def cost(flops, bytes_accessed):
    return pl.CostEstimate(flops=flops, bytes_accessed=bytes_accessed, transcendentals=0)


def params(mib):
    return pltpu.CompilerParams(vmem_limit_bytes=mib * 2**20)


def eliminate(flags, own_d, other_d, e, r):
    size, block = own_d.shape[0], BLOCK
    width = e.shape[1]
    return pl.pallas_call(
        eliminate_kernel,
        out_shape=(
            jax.ShapeDtypeStruct(e.shape, BF16),
            jax.ShapeDtypeStruct(r.shape, BF16),
            jax.ShapeDtypeStruct((width // 2, width // 2), BF16),
            jax.ShapeDtypeStruct((width // 2 + PAD, width // 2), BF16),
        ),
        in_specs=[SMEM, ANY, ANY, ANY, ANY],
        out_specs=(VMEM, VMEM, VMEM, VMEM),
        scratch_shapes=[
            pltpu.VMEM((size, size), BF16),
            pltpu.VMEM((size, size), F32),
            pltpu.VMEM(e.shape, BF16),
            pltpu.VMEM(r.shape, BF16),
            pltpu.VMEM(e.shape, F32),
            pltpu.VMEM(r.shape, F32),
            pltpu.VMEM((block, size), BF16),
            pltpu.VMEM((block, size), BF16),
            pltpu.VMEM((size, block), BF16),
            pltpu.VMEM((size, block), BF16),
            pltpu.VMEM((width, size), BF16),
            pltpu.VMEM((-(-(size // block) // 8) * 8, block), F32),
            pltpu.VMEM((block, block), F32),
            pltpu.VMEM((block, block), F32),
            pltpu.SemaphoreType.DMA((3, size // block)),
        ],
        compiler_params=params(52),
        cost_estimate=cost(28 * 10**9, 16 * 2**20),
    )(flags, own_d, other_d, e, r)


def tip_kernel(flags, own_r, other_r, out):
    width = own_r.shape[0]

    @pl.when(flags[0] == 0)
    def _():
        out[...] = jnp.zeros_like(out)

    @pl.when(jnp.logical_and(flags[0] != 0, flags[1] == 0))
    def _():
        out[0:width, :] = nt(own_r[...], other_r[...]).astype(BF16)
        out[width:, :] = jnp.zeros((out.shape[0] - width, width), BF16)

    @pl.when(jnp.logical_and(flags[0] != 0, flags[1] != 0))
    def _():
        first = nt(other_r[...], other_r[...])
        second = nt(own_r[...], own_r[...])
        folded, diagonal = fold(first, second, places(width))
        out[0:width, :] = folded.astype(BF16)
        out[width:, :] = jnp.broadcast_to(diagonal, (out.shape[0] - width, width)).astype(BF16)


def tip_term(flags, own_r, other_r):
    width = own_r.shape[0]
    return pl.pallas_call(
        tip_kernel,
        out_shape=jax.ShapeDtypeStruct((width + PAD, width), BF16),
        in_specs=[SMEM, VMEM, VMEM],
        out_specs=VMEM,
        compiler_params=params(16),
        cost_estimate=cost(10**9, 3 * 2**20),
    )(flags, own_r, other_r)


def arrow_kernel(flags, own_r, other_r, own_e, *outs):
    rows = own_r.shape[0]
    share = 2 * rows // len(outs)
    active, core = flags[2], flags[1]

    @pl.when(active == 0)
    def _():
        for out in outs:
            out[...] = jnp.zeros_like(out)

    def write(first, second):
        for source, base in ((first, 0), (second, rows)):
            value = (-nn(source[...], own_e[...])).astype(BF16)
            for i, out in enumerate(outs):
                low, high = max(base, i * share), min(base + rows, (i + 1) * share)
                if low < high:
                    out[low - i * share:high - i * share, :] = value[low - base:high - base, :]

    @pl.when(jnp.logical_and(active != 0, core == 0))
    def _():
        write(own_r, other_r)

    @pl.when(jnp.logical_and(active != 0, core != 0))
    def _():
        write(other_r, own_r)


def arrow_terms(flags, own_r, other_r, own_e):
    piece = jax.ShapeDtypeStruct((2 * own_r.shape[0] // PIECES, own_e.shape[1]), BF16)
    return pl.pallas_call(
        arrow_kernel,
        out_shape=(piece,) * PIECES,
        in_specs=[SMEM, VMEM, VMEM, VMEM],
        out_specs=(VMEM,) * PIECES,
        compiler_params=params(24),
        cost_estimate=cost(2 * 10**9, 6 * 2**20),
    )(flags, own_r, other_r, own_e)


def cross_kernel(flags, own_e, other_e, out):
    width = own_e.shape[1]
    half = width // 2

    @pl.when(flags[2] == 0)
    def _():
        out[...] = jnp.zeros_like(out)

    @pl.when(jnp.logical_and(flags[2] != 0, flags[1] == 0))
    def _():
        out[...] = nn(other_e[:, 0:half].T, own_e[...]).astype(BF16)

    @pl.when(jnp.logical_and(flags[2] != 0, flags[1] != 0))
    def _():
        out[...] = nn(own_e[:, half:width].T, other_e[...]).astype(BF16)


def cross_term(flags, own_e, other_e):
    width = own_e.shape[1]
    return pl.pallas_call(
        cross_kernel,
        out_shape=jax.ShapeDtypeStruct((width // 2, width), BF16),
        in_specs=[SMEM, VMEM, VMEM],
        out_specs=VMEM,
        compiler_params=params(24),
        cost_estimate=cost(2 * 10**9, 6 * 2**20),
    )(flags, own_e, other_e)


def separator_kernel(flags, separator, corner_in, folded, own_cross, other_cross, out):
    width = separator.shape[1]
    half = width // 2
    core = flags[1]
    first, second = unfold(
        folded[0:half, :].astype(F32), folded[half:half + 1, :].astype(F32), places(half)
    )
    corner = corner_in[...].astype(F32)
    base = pl.multiple_of(core * width, width)

    def less(rows, columns, term):
        out[rows, columns] = (separator[rows, columns].astype(F32) - term).astype(BF16)

    top, bottom = pl.ds(base, half), pl.ds(base + half, half)
    left, right = slice(0, half), slice(half, width)
    less(top, left, first)
    less(top, right, corner)
    less(bottom, left, corner.T)
    less(bottom, right, second)

    @pl.when(core == 0)
    def _():
        less(slice(width, width + half), slice(0, width), own_cross[...].astype(F32))
        less(slice(width + half, 2 * width), slice(0, width), other_cross[...].astype(F32))

    @pl.when(core != 0)
    def _():
        less(slice(0, width), left, other_cross[...].astype(F32).T)
        less(slice(0, width), right, own_cross[...].astype(F32).T)


def separator_less(flags, separator, corner, folded, own_cross, other_cross):
    return pl.pallas_call(
        separator_kernel,
        out_shape=jax.ShapeDtypeStruct(separator.shape, BF16),
        in_specs=[SMEM] + [VMEM] * 5,
        out_specs=VMEM,
        compiler_params=params(24),
        cost_estimate=cost(10**6, 6 * 2**20),
    )(flags, separator, corner, folded, own_cross, other_cross)


def new_tip_kernel(flags, tip, own_sum, other_sum, out):
    width = tip.shape[1]
    core = flags[1]

    @pl.when(core == 0)
    def _():
        first, _ = unfold(
            other_sum[0:width, :].astype(F32), other_sum[width:width + 1, :].astype(F32), places(width)
        )
        out[0:width, :] = tip[0:width, :].astype(F32) - first
        out[width:, :] = tip[width:, :].astype(F32) - own_sum[0:width, :].astype(F32).T

    @pl.when(core != 0)
    def _():
        _, second = unfold(
            own_sum[0:width, :].astype(F32), own_sum[width:width + 1, :].astype(F32), places(width)
        )
        out[0:width, :] = tip[0:width, :].astype(F32) - other_sum[0:width, :].astype(F32)
        out[width:, :] = tip[width:, :].astype(F32) - second


def tip_less(flags, tip, own_sum, other_sum):
    return pl.pallas_call(
        new_tip_kernel,
        out_shape=jax.ShapeDtypeStruct(tip.shape, F32),
        in_specs=[SMEM, VMEM, VMEM, VMEM],
        out_specs=VMEM,
        compiler_params=params(16),
        cost_estimate=cost(10**6, 3 * 2**20),
    )(flags, tip, own_sum, other_sum)


def rows_kernel(count, flags, *refs):
    sources, out, sem = refs[:count], refs[-2], refs[-1]
    share = sources[0].shape[0]

    def copy(source, i):
        place = out.at[i * share:(i + 1) * share, :]
        return pltpu.make_async_copy(source, place, sem.at[i])

    if count == 1:
        last = out.shape[0] // share - 1
        copy(sources[0], last).start()
        copy(sources[0], last).wait()
        return

    @pl.when(flags[3] == 0)
    def _():
        copy(sources[0], 0).start()

    @pl.when(flags[3] != 0)
    def _():
        copy(sources[1], 0).start()

    for i, source in enumerate(sources[2:]):
        copy(source, i + 1).start()
    for i, source in enumerate(sources[1:]):
        copy(source, i).wait()


def rows_placed(flags, pieces, whole):
    count = len(pieces)
    shape = whole if isinstance(whole, tuple) else whole.shape
    more = () if isinstance(whole, tuple) else (whole,)
    return pl.pallas_call(
        functools.partial(rows_kernel, count),
        out_shape=jax.ShapeDtypeStruct(shape, BF16),
        in_specs=[SMEM] + [VMEM] * count + [ANY] * len(more),
        out_specs=ANY,
        scratch_shapes=[pltpu.SemaphoreType.DMA((PIECES,))],
        input_output_aliases={count + 1: 0} if more else {},
        compiler_params=params(16),
        cost_estimate=cost(10**6, 2 * 2**20),
    )(flags, *pieces, *more)


def swapped(x):
    return lax.ppermute(x, "space", [(0, 1), (1, 0)])


def to_previous(x):
    count = lax.axis_size("tm")
    return lax.ppermute(x, "tm", [(i, i - 1) for i in range(1, count)])


def from_every_other(x, first):
    count = lax.axis_size("tm")
    return lax.ppermute(x, "tm", [(i, i - 1) for i in range(first, count, 2)])


def added(*terms):
    return sum(term.astype(F32) for term in terms).astype(BF16)


def summed(term):
    count = lax.axis_size("tm")
    term = added(term, lax.ppermute(term, "tm", [(i, i + 1) for i in range(0, count, 2)]))
    distance = 2
    while distance < count:
        pairs = [(i, i ^ distance) for i in range(1, count, 2)]
        term = added(term, lax.ppermute(term, "tm", pairs))
        distance *= 2
    returned = lax.ppermute(term, "tm", [(i + 1, i) for i in range(0, count, 2)])
    return jnp.where(lax.axis_index("tm") % 2 == 0, returned, term)


def on_device(interior_diag, coupling, arrow_rows, separator_diag, tip, lengths):
    position = lax.axis_index("tm")
    active = lengths[position] == 2
    flags = jnp.stack(
        [
            active,
            lax.axis_index("space") != 0,
            jnp.logical_and(active, position != 0),
            position % 2 != 0,
        ]
    ).astype(jnp.int32)
    other_diag = swapped(interior_diag)
    own_e, own_r, corner, folded = eliminate(flags, interior_diag, other_diag, coupling, arrow_rows)
    corner = to_previous(corner)
    other_r = swapped(own_r)
    term = tip_term(flags, own_r, other_r)
    tip_sum = summed(term)
    folded = to_previous(folded)
    other_e = swapped(own_e)
    cross = cross_term(flags, own_e, other_e)
    cross = to_previous(cross)
    pieces = arrow_terms(flags, own_r, other_r, own_e)
    received = [from_every_other(pieces[0], 1)]
    received.append(from_every_other(pieces[0], 2))
    for piece in pieces[1:]:
        received.append(to_previous(piece))
    arrow_fill = rows_placed(
        flags, received[:-1], (2 * own_r.shape[0], own_e.shape[1])
    )
    arrow_fill = rows_placed(flags, received[-1:], arrow_fill)
    other_cross = swapped(cross)
    new_separator = separator_less(flags, separator_diag, corner, folded, cross, other_cross)
    other_sum = swapped(tip_sum)
    new_tip = tip_less(flags, tip, tip_sum, other_sum)
    return (new_separator, arrow_fill, new_tip)


def solution(mesh):
    return jax.shard_map(
        on_device,
        mesh=mesh,
        in_specs=(
            P(("groups", "tm"), "space"),
            P(("groups", "tm"), "space"),
            P(("groups", "tm", "space"), None),
            P(("groups", "tm"), "space"),
            P("groups", "space"),
            P("groups"),
        ),
        out_specs=(
            P(("groups", "tm"), "space"),
            P(("groups", "tm"), "space"),
            P("groups", "space"),
        ),
        check_vma=False,
    )
```

```python
import functools

import jax
import jax.numpy as jnp
from jax import lax
from jax.experimental import pallas as pl
from jax.experimental.pallas import tpu as pltpu
from jax.sharding import PartitionSpec as P


F32 = jnp.float32
BF16 = jnp.bfloat16
BLOCK = 256
NEAR = 0.03
MOST_STEPS = 60
STAGES = 7
PAD = 16
PIECES = (3, 2, 1)


def split(x):
    high = x.astype(BF16)
    return high, (x - high.astype(F32)).astype(BF16)


def nn(a, b):
    return lax.dot_general(a, b, (((1,), (0,)), ((), ())), preferred_element_type=F32)


def nt(a, b):
    return lax.dot_general(a, b, (((1,), (1,)), ((), ())), preferred_element_type=F32)


def three(dot, a, b):
    return dot(a[0], b[0]) + (dot(a[0], b[1]) + dot(a[1], b[0]))


def total(x):
    return jnp.sum(x, keepdims=True)


def places(size):
    rows = lax.broadcasted_iota(jnp.int32, (size, size), 0)
    columns = lax.broadcasted_iota(jnp.int32, (size, size), 1)
    return rows, columns


def diagonal_row(x, on_diagonal):
    return jnp.sum(jnp.where(on_diagonal, x, 0.0), axis=0, keepdims=True)


def unit_scaled(a, on_diagonal):
    diagonal = jnp.where(on_diagonal, a, 0.0)
    scale_row = lax.rsqrt(jnp.sum(diagonal, axis=0, keepdims=True))
    scale_column = lax.rsqrt(jnp.sum(diagonal, axis=1, keepdims=True))
    return a * scale_row * scale_column, scale_row


def first_root(off, off_square, identity):
    bound = jnp.sqrt(jnp.sqrt(total(off_square * off_square)))
    c = jnp.minimum(1.0, 1.9 / (1.0 + bound))
    gap = c * off - (1.0 - c) * identity
    gap_square = c * c * off_square - (2 * c * (1 - c)) * off + ((1 - c) * (1 - c)) * identity
    return (jnp.sqrt(c) * (identity - 0.5 * gap + 0.375 * gap_square)).astype(BF16)


def root_stages(a, on_diagonal, identity, result):
    unit, scale_row = unit_scaled(a, on_diagonal)
    off = unit - identity
    off_high = off.astype(BF16)
    high, low = split(unit)
    yield
    off_square = nn(off_high, off_high)
    yield
    first = first_root(off, off_square, identity)
    yield
    product = split(nt(high, first) + nt(low, first))
    yield
    gap = nn(first, product[0]) + nn(first, product[1]) - identity
    gap_high = gap.astype(BF16)
    yield
    gap_square = nn(gap_high, gap_high)
    change = split(0.375 * gap_square - 0.5 * gap)
    yield
    root = first.astype(F32) + (nn(change[0], first) + nn(change[1], first))
    result.append(split(root * scale_row))
    result.append(gap_square)


def root_until_near(a, on_diagonal, identity, unit_ref, root_ref):
    unit, scale_row = unit_scaled(a, on_diagonal)
    off = unit - identity
    off_square = nn(off.astype(BF16), off.astype(BF16))
    unit_ref[...] = unit
    root_ref[...] = first_root(off, off_square, identity).astype(F32)

    def far(state):
        return jnp.logical_and(jnp.logical_not(state[0] <= NEAR**4), state[1] < MOST_STEPS)

    def step(state):
        root = split(root_ref[...])
        product = split(three(nt, split(unit_ref[...]), root))
        gap = three(nn, root, product) - identity
        gap_square = nn(gap.astype(BF16), gap.astype(BF16))
        change = split(0.375 * gap_square - 0.5 * gap)
        root_ref[...] += three(nn, change, root)
        return jnp.sum(gap_square * gap_square), state[1] + 1

    lax.while_loop(far, step, (jnp.float32(1.0), jnp.int32(0)))
    return split(root_ref[...] * scale_row)


def interleave(stages, fillers):
    share = -(-len(fillers) // STAGES)
    for _ in stages:
        for filler in fillers[:share]:
            filler()
        fillers = fillers[share:]
    for filler in fillers:
        filler()


def eliminate_kernel(
    flags, own_d, other_d, e_hbm, r_hbm, solved_e, solved_r, corner_out, folded_out,
    given, diag, e_in, r_in, left_e, left_r, high, low, high_t, low_t, turned,
    near, unit_ref, root_ref, sems,
):
    size, block = diag.shape[0], unit_ref.shape[0]
    half, width = own_d.shape[1], e_in.shape[1]
    steps = size // block
    core = flags[1]

    def at(i):
        return slice(i * block, (i + 1) * block)

    def arrival(i, which):
        source = own_d if which == 0 else other_d
        side = core if which == 0 else 1 - core
        columns = pl.ds(pl.multiple_of(side * half, half), half)
        return pltpu.make_async_copy(source.at[at(i), :], given.at[at(i), columns], sems.at[which, i])

    rows, columns = places(block)
    on_diagonal = rows == columns
    identity = jnp.where(on_diagonal, 1.0, 0.0).astype(F32)
    e_copy = pltpu.make_async_copy(e_hbm, e_in, sems.at[2, 0])
    r_copy = pltpu.make_async_copy(r_hbm, r_in, sems.at[2, 1])

    @pl.when(flags[0] == 0)
    def _():
        solved_e[...] = jnp.zeros_like(solved_e)
        solved_r[...] = jnp.zeros_like(solved_r)
        corner_out[...] = jnp.zeros_like(corner_out)
        folded_out[...] = jnp.zeros_like(folded_out)

    @pl.when(flags[0] != 0)
    def _():
        for i in range(steps):
            arrival(i, 0).start()
            arrival(i, 1).start()
        r_copy.start()
        e_copy.start()

        def take(i):
            arrival(i, 0).wait()
            arrival(i, 1).wait()
            diag[at(i), i * block:] = given[at(i), i * block:].astype(F32)

        def take_r():
            r_copy.wait()
            left_r[...] = r_in[...].astype(F32)

        def take_e():
            e_copy.wait()
            left_e[...] = e_in[...].astype(F32)

        take(0)
        result = []
        fillers = [functools.partial(take, i) for i in range(1, steps)] + [take_r, take_e]
        interleave(root_stages(diag[at(0), at(0)], on_diagonal, identity, result), fillers)
        for k in range(steps):
            root, gap_square = result
            near[k:k + 1, :] = jnp.sum(gap_square * gap_square, axis=0, keepdims=True)
            result, part_e, part_r = [], [], []

            def panel(j):
                value = three(nn, root, split(diag[at(k), at(j)]))
                high[:, at(j)], low[:, at(j)] = split(value)
                high_t[at(j), :], low_t[at(j), :] = split(value.T)

            def update(i, j):
                left = (high_t[at(i), :], low_t[at(i), :])
                diag[at(i), at(j)] -= three(nn, left, (high[:, at(j)], low[:, at(j)]))

            def solve_r():
                part_r.extend(split(three(nt, split(left_r[:, at(k)]), root)))
                solved_r[:, at(k)] = part_r[0]

            def update_r(i):
                left_r[:, at(i)] -= three(nn, part_r, (high[:, at(i)], low[:, at(i)]))

            def solve_e():
                value = three(nn, root, split(left_e[at(k), :]))
                part_e.extend(split(value))
                solved_e[at(k), :] = part_e[0]
                turned[:, at(k)] = value.T.astype(BF16)

            def update_e(i):
                left_e[at(i), :] -= three(nn, (high_t[at(i), :], low_t[at(i), :]), part_e)

            fillers = [functools.partial(panel, j) for j in range(k + 2, steps)]
            fillers += [
                functools.partial(update, i, j)
                for i in range(k + 1, steps) for j in range(max(i, k + 2), steps)
            ]
            fillers.append(solve_e)
            fillers += [functools.partial(update_e, i) for i in range(k + 1, steps)]
            fillers.append(solve_r)
            fillers += [functools.partial(update_r, i) for i in range(k + 1, steps)]
            if k + 1 < steps:
                panel(k + 1)
                update(k + 1, k + 1)
                stages = root_stages(diag[at(k + 1), at(k + 1)], on_diagonal, identity, result)
                interleave(stages, fillers)
            else:
                interleave((), fillers)
        worst = jnp.max(jnp.sum(near[0:steps, :], axis=1, keepdims=True))

        @pl.when(jnp.logical_not(worst <= NEAR**4))
        def _():
            for i in range(steps):
                diag[at(i), i * block:] = given[at(i), i * block:].astype(F32)
            left_e[...] = e_in[...].astype(F32)
            left_r[...] = r_in[...].astype(F32)

            def spot(i):
                return pl.ds(pl.multiple_of(i * block, block), block)

            def eliminate(k, carry):
                now = spot(k)
                root = root_until_near(diag[now, now], on_diagonal, identity, unit_ref, root_ref)
                part_r = split(three(nt, split(left_r[:, now]), root))
                solved_r[:, now] = part_r[0]

                value = three(nn, root, split(left_e[now, :]))
                part_e = split(value)
                solved_e[now, :] = part_e[0]
                turned[:, now] = value.T.astype(BF16)

                def panel(j, carry):
                    there = spot(j)
                    value = three(nn, root, split(diag[now, there]))
                    high[:, there], low[:, there] = split(value)
                    high_t[there, :], low_t[there, :] = split(value.T)
                    left_r[:, there] -= three(nn, part_r, (high[:, there], low[:, there]))
                    left = (high_t[there, :], low_t[there, :])
                    left_e[there, :] -= three(nn, left, part_e)
                    return carry

                def row(i, carry):
                    here = spot(i)
                    left = (high_t[here, :], low_t[here, :])

                    def update(j, carry):
                        there = spot(j)
                        diag[here, there] -= three(nn, left, (high[:, there], low[:, there]))
                        return carry

                    return lax.fori_loop(i, steps, update, carry)

                lax.fori_loop(k + 1, steps, panel, 0)
                lax.fori_loop(k + 1, steps, row, 0)
                return carry

            lax.fori_loop(0, steps, eliminate, 0)

        corner = width // 2
        first = nn(turned[0:corner, :], solved_e[:, 0:corner])
        second = nn(turned[corner:width, :], solved_e[:, corner:width])
        folded, diagonal = fold(first, second, places(corner))
        folded_out[0:corner, :] = folded.astype(BF16)
        folded_out[corner:, :] = jnp.broadcast_to(diagonal, (PAD, corner)).astype(BF16)
        corner_out[...] = nn(turned[0:corner, :], solved_e[:, corner:width]).astype(BF16)


def fold(first, second, strict):
    rows, columns = strict
    return jnp.where(rows <= columns, first, second), diagonal_row(second, rows == columns)


def unfold(folded, diagonal, strict):
    rows, columns = strict
    turned = folded.T
    first = jnp.where(rows <= columns, folded, turned)
    second = jnp.where(rows > columns, folded, jnp.where(rows < columns, turned, diagonal))
    return first, second


ANY = pl.BlockSpec(memory_space=pl.ANY)
VMEM = pl.BlockSpec(memory_space=pltpu.VMEM)
SMEM = pl.BlockSpec(memory_space=pltpu.SMEM)


def cost(flops, bytes_accessed):
    return pl.CostEstimate(flops=flops, bytes_accessed=bytes_accessed, transcendentals=0)


def params(mib):
    return pltpu.CompilerParams(vmem_limit_bytes=mib * 2**20)


def eliminate(flags, own_d, other_d, e, r):
    size, block = own_d.shape[0], BLOCK
    width = e.shape[1]
    return pl.pallas_call(
        eliminate_kernel,
        out_shape=(
            jax.ShapeDtypeStruct(e.shape, BF16),
            jax.ShapeDtypeStruct(r.shape, BF16),
            jax.ShapeDtypeStruct((width // 2, width // 2), BF16),
            jax.ShapeDtypeStruct((width // 2 + PAD, width // 2), BF16),
        ),
        in_specs=[SMEM, ANY, ANY, ANY, ANY],
        out_specs=(VMEM, VMEM, VMEM, VMEM),
        scratch_shapes=[
            pltpu.VMEM((size, size), BF16),
            pltpu.VMEM((size, size), F32),
            pltpu.VMEM(e.shape, BF16),
            pltpu.VMEM(r.shape, BF16),
            pltpu.VMEM(e.shape, F32),
            pltpu.VMEM(r.shape, F32),
            pltpu.VMEM((block, size), BF16),
            pltpu.VMEM((block, size), BF16),
            pltpu.VMEM((size, block), BF16),
            pltpu.VMEM((size, block), BF16),
            pltpu.VMEM((width, size), BF16),
            pltpu.VMEM((-(-(size // block) // 8) * 8, block), F32),
            pltpu.VMEM((block, block), F32),
            pltpu.VMEM((block, block), F32),
            pltpu.SemaphoreType.DMA((3, size // block)),
        ],
        compiler_params=params(52),
        cost_estimate=cost(28 * 10**9, 16 * 2**20),
    )(flags, own_d, other_d, e, r)


def tip_kernel(flags, own_r, other_r, out):
    width = own_r.shape[0]

    @pl.when(flags[0] == 0)
    def _():
        out[...] = jnp.zeros_like(out)

    @pl.when(jnp.logical_and(flags[0] != 0, flags[1] == 0))
    def _():
        out[0:width, :] = nt(own_r[...], other_r[...]).astype(BF16)
        out[width:, :] = jnp.zeros((out.shape[0] - width, width), BF16)

    @pl.when(jnp.logical_and(flags[0] != 0, flags[1] != 0))
    def _():
        first = nt(other_r[...], other_r[...])
        second = nt(own_r[...], own_r[...])
        folded, diagonal = fold(first, second, places(width))
        out[0:width, :] = folded.astype(BF16)
        out[width:, :] = jnp.broadcast_to(diagonal, (out.shape[0] - width, width)).astype(BF16)


def tip_term(flags, own_r, other_r):
    width = own_r.shape[0]
    return pl.pallas_call(
        tip_kernel,
        out_shape=jax.ShapeDtypeStruct((width + PAD, width), BF16),
        in_specs=[SMEM, VMEM, VMEM],
        out_specs=VMEM,
        compiler_params=params(16),
        cost_estimate=cost(10**9, 3 * 2**20),
    )(flags, own_r, other_r)


def starts(rows):
    return [sum(PIECES[:i]) * rows // sum(PIECES) for i in range(len(PIECES) + 1)]


def arrow_kernel(flags, own_r, other_r, own_e, *outs):
    rows = own_r.shape[0]
    bounds = starts(2 * rows)
    active, core = flags[2], flags[1]

    @pl.when(active == 0)
    def _():
        for out in outs:
            out[...] = jnp.zeros_like(out)

    def write(first, second):
        for source, base in ((first, 0), (second, rows)):
            value = (-nn(source[...], own_e[...])).astype(BF16)
            for i, out in enumerate(outs):
                begin = bounds[i]
                low, high = max(base, begin), min(base + rows, bounds[i + 1])
                if low < high:
                    out[low - begin:high - begin, :] = value[low - base:high - base, :]

    @pl.when(jnp.logical_and(active != 0, core == 0))
    def _():
        write(own_r, other_r)

    @pl.when(jnp.logical_and(active != 0, core != 0))
    def _():
        write(other_r, own_r)


def arrow_terms(flags, own_r, other_r, own_e):
    bounds = starts(2 * own_r.shape[0])
    return pl.pallas_call(
        arrow_kernel,
        out_shape=tuple(
            jax.ShapeDtypeStruct((high - low, own_e.shape[1]), BF16)
            for low, high in zip(bounds, bounds[1:])
        ),
        in_specs=[SMEM, VMEM, VMEM, VMEM],
        out_specs=(VMEM,) * len(PIECES),
        compiler_params=params(24),
        cost_estimate=cost(2 * 10**9, 6 * 2**20),
    )(flags, own_r, other_r, own_e)


def cross_kernel(flags, own_e, other_e, out):
    width = own_e.shape[1]
    half = width // 2

    @pl.when(flags[2] == 0)
    def _():
        out[...] = jnp.zeros_like(out)

    @pl.when(jnp.logical_and(flags[2] != 0, flags[1] == 0))
    def _():
        out[...] = nn(other_e[:, 0:half].T, own_e[...]).astype(BF16)

    @pl.when(jnp.logical_and(flags[2] != 0, flags[1] != 0))
    def _():
        out[...] = nn(own_e[:, half:width].T, other_e[...]).astype(BF16)


def cross_term(flags, own_e, other_e):
    width = own_e.shape[1]
    return pl.pallas_call(
        cross_kernel,
        out_shape=jax.ShapeDtypeStruct((width // 2, width), BF16),
        in_specs=[SMEM, VMEM, VMEM],
        out_specs=VMEM,
        compiler_params=params(24),
        cost_estimate=cost(2 * 10**9, 6 * 2**20),
    )(flags, own_e, other_e)


def separator_kernel(flags, separator, corner_in, folded, own_cross, other_cross, out):
    width = separator.shape[1]
    half = width // 2
    core = flags[1]
    first, second = unfold(
        folded[0:half, :].astype(F32), folded[half:half + 1, :].astype(F32), places(half)
    )
    corner = corner_in[...].astype(F32)
    base = pl.multiple_of(core * width, width)

    def less(rows, columns, term):
        out[rows, columns] = (separator[rows, columns].astype(F32) - term).astype(BF16)

    top, bottom = pl.ds(base, half), pl.ds(base + half, half)
    left, right = slice(0, half), slice(half, width)
    less(top, left, first)
    less(top, right, corner)
    less(bottom, left, corner.T)
    less(bottom, right, second)

    @pl.when(core == 0)
    def _():
        less(slice(width, width + half), slice(0, width), own_cross[...].astype(F32))
        less(slice(width + half, 2 * width), slice(0, width), other_cross[...].astype(F32))

    @pl.when(core != 0)
    def _():
        less(slice(0, width), left, other_cross[...].astype(F32).T)
        less(slice(0, width), right, own_cross[...].astype(F32).T)


def separator_less(flags, separator, corner, folded, own_cross, other_cross):
    return pl.pallas_call(
        separator_kernel,
        out_shape=jax.ShapeDtypeStruct(separator.shape, BF16),
        in_specs=[SMEM] + [VMEM] * 5,
        out_specs=VMEM,
        compiler_params=params(24),
        cost_estimate=cost(10**6, 6 * 2**20),
    )(flags, separator, corner, folded, own_cross, other_cross)


def new_tip_kernel(flags, tip, own_sum, other_sum, out):
    width = tip.shape[1]
    core = flags[1]

    @pl.when(core == 0)
    def _():
        first, _ = unfold(
            other_sum[0:width, :].astype(F32), other_sum[width:width + 1, :].astype(F32), places(width)
        )
        out[0:width, :] = tip[0:width, :].astype(F32) - first
        out[width:, :] = tip[width:, :].astype(F32) - own_sum[0:width, :].astype(F32).T

    @pl.when(core != 0)
    def _():
        _, second = unfold(
            own_sum[0:width, :].astype(F32), own_sum[width:width + 1, :].astype(F32), places(width)
        )
        out[0:width, :] = tip[0:width, :].astype(F32) - other_sum[0:width, :].astype(F32)
        out[width:, :] = tip[width:, :].astype(F32) - second


def tip_less(flags, tip, own_sum, other_sum):
    return pl.pallas_call(
        new_tip_kernel,
        out_shape=jax.ShapeDtypeStruct(tip.shape, F32),
        in_specs=[SMEM, VMEM, VMEM, VMEM],
        out_specs=VMEM,
        compiler_params=params(16),
        cost_estimate=cost(10**6, 3 * 2**20),
    )(flags, tip, own_sum, other_sum)


def rows_kernel(count, flags, *refs):
    sources, out, sem = refs[:count], refs[-2], refs[-1]
    bounds = starts(out.shape[0])

    def copy(source, i):
        place = out.at[bounds[i]:bounds[i + 1], :]
        return pltpu.make_async_copy(source, place, sem.at[i])

    if count == 1:
        last = len(PIECES) - 1
        copy(sources[0], last).start()
        copy(sources[0], last).wait()
        return

    @pl.when(flags[3] == 0)
    def _():
        copy(sources[0], 0).start()

    @pl.when(flags[3] != 0)
    def _():
        copy(sources[1], 0).start()

    for i, source in enumerate(sources[2:]):
        copy(source, i + 1).start()
    for i, source in enumerate(sources[1:]):
        copy(source, i).wait()


def rows_placed(flags, pieces, whole):
    count = len(pieces)
    shape = whole if isinstance(whole, tuple) else whole.shape
    more = () if isinstance(whole, tuple) else (whole,)
    return pl.pallas_call(
        functools.partial(rows_kernel, count),
        out_shape=jax.ShapeDtypeStruct(shape, BF16),
        in_specs=[SMEM] + [VMEM] * count + [ANY] * len(more),
        out_specs=ANY,
        scratch_shapes=[pltpu.SemaphoreType.DMA((len(PIECES),))],
        input_output_aliases={count + 1: 0} if more else {},
        compiler_params=params(16),
        cost_estimate=cost(10**6, 2 * 2**20),
    )(flags, *pieces, *more)


def swapped(x):
    return lax.ppermute(x, "space", [(0, 1), (1, 0)])


def to_previous(x):
    count = lax.axis_size("tm")
    return lax.ppermute(x, "tm", [(i, i - 1) for i in range(1, count)])


def from_every_other(x, first):
    count = lax.axis_size("tm")
    return lax.ppermute(x, "tm", [(i, i - 1) for i in range(first, count, 2)])


def added(*terms):
    return sum(term.astype(F32) for term in terms).astype(BF16)


def summed(term):
    count = lax.axis_size("tm")
    term = added(term, lax.ppermute(term, "tm", [(i, i + 1) for i in range(0, count, 2)]))
    distance = 2
    while distance < count:
        pairs = [(i, i ^ distance) for i in range(1, count, 2)]
        term = added(term, lax.ppermute(term, "tm", pairs))
        distance *= 2
    returned = lax.ppermute(term, "tm", [(i + 1, i) for i in range(0, count, 2)])
    return jnp.where(lax.axis_index("tm") % 2 == 0, returned, term)


def on_device(interior_diag, coupling, arrow_rows, separator_diag, tip, lengths):
    position = lax.axis_index("tm")
    active = lengths[position] == 2
    flags = jnp.stack(
        [
            active,
            lax.axis_index("space") != 0,
            jnp.logical_and(active, position != 0),
            position % 2 != 0,
        ]
    ).astype(jnp.int32)
    other_diag = swapped(interior_diag)
    own_e, own_r, corner, folded = eliminate(flags, interior_diag, other_diag, coupling, arrow_rows)
    corner = to_previous(corner)
    other_r = swapped(own_r)
    term = tip_term(flags, own_r, other_r)
    tip_sum = summed(term)
    folded = to_previous(folded)
    other_e = swapped(own_e)
    cross = cross_term(flags, own_e, other_e)
    cross = to_previous(cross)
    pieces = arrow_terms(flags, own_r, other_r, own_e)
    received = [from_every_other(pieces[0], 1)]
    received.append(from_every_other(pieces[0], 2))
    for piece in pieces[1:]:
        received.append(to_previous(piece))
    arrow_fill = rows_placed(
        flags, received[:-1], (2 * own_r.shape[0], own_e.shape[1])
    )
    arrow_fill = rows_placed(flags, received[-1:], arrow_fill)
    other_cross = swapped(cross)
    new_separator = separator_less(flags, separator_diag, corner, folded, cross, other_cross)
    other_sum = swapped(tip_sum)
    new_tip = tip_less(flags, tip, tip_sum, other_sum)
    return (new_separator, arrow_fill, new_tip)


def solution(mesh):
    return jax.shard_map(
        on_device,
        mesh=mesh,
        in_specs=(
            P(("groups", "tm"), "space"),
            P(("groups", "tm"), "space"),
            P(("groups", "tm", "space"), None),
            P(("groups", "tm"), "space"),
            P("groups", "space"),
            P("groups"),
        ),
        out_specs=(
            P(("groups", "tm"), "space"),
            P(("groups", "tm"), "space"),
            P("groups", "space"),
        ),
        check_vma=False,
    )
```
